32 devices in a mesh: fsdp: 32 (over z, y, x, core).
Axes of the slice: x: 2, y: 2, z: 4, core: 2. Of those that a mesh axis runs over, the one named last changes fastest.
Arguments:
- block_input: float32 [4096, 1024], P('fsdp'), may hold values from -12 to 12
- ln1_gain: bfloat16 [1024], P('fsdp'), may hold values from 0.5 to 1.5
- ln1_bias: bfloat16 [1024], P('fsdp'), may hold values from -3 to 3
- w_qkv: bfloat16 [1024, 3072], P('fsdp'), may hold values from -0.1875 to 0.1875
- bias_qv: bfloat16 [2048], P('fsdp'), may hold values from -3 to 3
- w_out: bfloat16 [1024, 1024], P('fsdp'), may hold values from -0.75 to 0.75
- bias_out: bfloat16 [1024], P('fsdp'), may hold values from -3 to 3
- ln2_gain: bfloat16 [1024], P('fsdp'), may hold values from 0.5 to 1.5
- ln2_bias: bfloat16 [1024], P('fsdp'), may hold values from -3 to 3
- w_fc: bfloat16 [1024, 4096], P('fsdp'), may hold values from -0.1875 to 0.1875
- bias_fc: bfloat16 [4096], P('fsdp'), may hold values from -3 to 3
- w_proj: bfloat16 [4096, 1024], P('fsdp'), may hold values from -0.09375 to 0.09375
- bias_proj: bfloat16 [1024], P('fsdp'), may hold values from -3 to 3
- seq_lengths: int32 [16], replicated, may hold values from 1 to 512, 4096 in all
- out_grad: float32 [4096, 1024], P('fsdp'), may hold values from -12 to 12
Outputs:
- block_output: float32 [4096, 1024], P('fsdp')
- grad_input: float32 [4096, 1024], P('fsdp')
- grad_ln1_gain: float32 [1024], P('fsdp')
- grad_ln1_bias: float32 [1024], P('fsdp')
- grad_w_qkv: float32 [1024, 3072], P('fsdp')
- grad_bias_qv: float32 [2048], P('fsdp')
- grad_w_out: float32 [1024, 1024], P('fsdp')
- grad_bias_out: float32 [1024], P('fsdp')
- grad_ln2_gain: float32 [1024], P('fsdp')
- grad_ln2_bias: float32 [1024], P('fsdp')
- grad_w_fc: float32 [1024, 4096], P('fsdp')
- grad_bias_fc: float32 [4096], P('fsdp')
- grad_w_proj: float32 [4096, 1024], P('fsdp')
- grad_bias_proj: float32 [1024], P('fsdp')
The draws below stay inside these ranges and needn't reach their ends.
Inputs may be any that keep to these rules, and one draw needn't show every extreme that they name: `seq_lengths`: sequences lie end to end in token order: sequence s begins after the sum of the lengths before it. The lengths sum to 4096 and the largest is exactly 512.
All inputs are finite; a program needn't handle non-finite values.
Results may differ from the reference program's by a relative error of at most 0.0095.
Values may be sent and summed in bfloat16 or wider, within the bound.
No kernel may reach another device: no remote copies, remote signals or barrier semaphores. Data moves between devices by JAX's collectives and lax.ppermute only.
A program may use at most 256 MiB of HBM per device.

```python
import math
import jax
import jax.numpy as jnp
import numpy as np
from jax import lax

D = 1024
HEADS = 16
HEAD_DIM = 64
FF = 4096
MAXLEN = 512
TOKENS = 4096
SEQS = 16


def strengthened(entries, key, source, target, blocks, factor):
    def block_of(axis_at):
        return (jnp.arange(entries.shape[axis_at]) // (entries.shape[axis_at] // blocks)).reshape((-1,) + (1,) * (entries.ndim - 1 - axis_at))

    near = jax.random.permutation(key, blocks)[block_of(target)]
    other_side = (block_of(target) + blocks // 2) % blocks
    return jnp.where((block_of(source) == near) | (block_of(source) == other_side), factor * entries, entries)


def block_levels(own_key, extent, shards, least, high):
    loudness = 1.0
    for position, parts in shards:
        steps = jax.random.uniform(jax.random.fold_in(jax.random.fold_in(own_key, 6), position), (parts,), jnp.float32, least / len(shards), high / len(shards))
        loudness = loudness * jnp.repeat(jnp.exp(steps), extent[position] // parts).reshape((-1,) + (1,) * (len(extent) - 1 - position))
    return loudness


def profile(count, total, most, slope):
    weights = [(1 << 20) // math.isqrt(rank ** slope) + 1 for rank in range(2, count + 1)]
    spare, counts = total - most - (count - 1), [1] * (count - 1)
    while spare > 0:
        free = [i for i in range(count - 1) if counts[i] < most]
        mass, budget = sum([weights[i] for i in free]), spare
        for i in free:
            addition = min(most - counts[i], max(1, budget * weights[i] // mass), spare)
            counts[i] = counts[i] + addition
            spare = spare - addition
    return np.array([most] + counts)


def ragged(key, amount, total, bound, lean):
    if amount == 2:
        one = jax.random.randint(key, (), max(1, total - bound), min(bound, total - 1) + 1)
        return jnp.stack([one, total - one])
    lengths = jnp.asarray(profile(amount, total, bound, lean), jnp.int32)
    pairs = (amount - 1) // 2
    source_of, sink = lengths[1:1 + 2 * pairs:2], lengths[2:2 + 2 * pairs:2]
    room = jnp.minimum(source_of - 1, bound - sink)
    moved = jax.random.randint(jax.random.fold_in(key, 1), (pairs,), 0, 1 << 20) % (room + 1)
    lengths = lengths.at[1:1 + 2 * pairs:2].set(source_of - moved).at[2:2 + 2 * pairs:2].set(sink + moved)
    return lengths[jax.random.permutation(jax.random.fold_in(key, 2), amount)]


def scatter_about(rng, extent, scale, reach, shards=(), kind=jnp.bfloat16):
    drawn = scale * jax.random.normal(rng, extent, jnp.float32)
    if shards:
        drawn = drawn * block_levels(rng, extent, shards, -0.22, 0.18)
    return jnp.clip(drawn, -reach, reach).astype(kind)


def gaussian_with(own_key, dims, spread, limit, shards, heavy, held_as=jnp.bfloat16):
    drawn = spread * jax.random.normal(own_key, dims, jnp.float32)
    if shards:
        drawn = drawn * block_levels(own_key, dims, shards, -0.22, 0.18)
    return jnp.clip(strengthened(drawn, jax.random.fold_in(own_key, 3), *heavy), -limit, limit).astype(held_as)


def setup_inputs(seed: int = 0) -> dict:
    seeds = jax.random.split(jax.random.key(seed), 16)
    block_input = gaussian_with(seeds[0], (TOKENS, D), 1.0, 12.0, ((0, 32),), (0, 1, 32, 2.75), jnp.float32)
    ln1_gain = jnp.clip(1.0 + 0.1 * jax.random.normal(seeds[1], (D,), jnp.float32), 0.5, 1.5).astype(jnp.bfloat16)
    ln1_bias = scatter_about(seeds[2], (D,), 0.5, 3.0, ((0, 32),))
    w_qkv = scatter_about(seeds[3], (D, 3 * D), D ** -0.5, 0.1875, ((0, 32),))
    bias_qv = scatter_about(seeds[4], (2 * D,), 0.3, 3.0, ((0, 32),))
    w_out = scatter_about(seeds[5], (D, D), (D // 16) ** -0.5, 0.75, ((0, 32),))
    bias_out = scatter_about(seeds[6], (D,), 0.3, 3.0, ((0, 32),))
    ln2_gain = jnp.clip(1.0 + 0.1 * jax.random.normal(seeds[7], (D,), jnp.float32), 0.5, 1.5).astype(jnp.bfloat16)
    ln2_bias = scatter_about(seeds[8], (D,), 0.5, 3.0, ((0, 32),))
    w_fc = scatter_about(seeds[9], (D, FF), D ** -0.5, 0.1875, ((0, 32),))
    bias_fc = scatter_about(seeds[10], (FF,), 0.5, 3.0, ((0, 32),))
    w_proj = scatter_about(seeds[11], (FF, D), FF ** -0.5, 0.09375, ((0, 32),))
    bias_proj = scatter_about(seeds[12], (D,), 0.3, 3.0, ((0, 32),))
    seq_lengths = ragged(seeds[13], SEQS, TOKENS, MAXLEN, 2).astype(jnp.int32)
    out_grad = gaussian_with(seeds[14], (TOKENS, D), 1.0, 12.0, ((0, 32),), (0, 1, 32, 2.75), jnp.float32)
    return {"block_input": block_input, "ln1_gain": ln1_gain, "ln1_bias": ln1_bias, "w_qkv": w_qkv, "bias_qv": bias_qv, "w_out": w_out, "bias_out": bias_out, "ln2_gain": ln2_gain, "ln2_bias": ln2_bias, "w_fc": w_fc, "bias_fc": bias_fc, "w_proj": w_proj, "bias_proj": bias_proj, "seq_lengths": seq_lengths, "out_grad": out_grad}


EPSILON = 1e-05
GELU_C = math.sqrt(2.0 / math.pi)
MASKED = -1e+30

def layer_norm(values, gain, shift_bias):
    row_mean = lax.optimization_barrier(jnp.mean(values, axis=-1, keepdims=True))
    centred = values - row_mean
    row_var = lax.optimization_barrier(jnp.mean(centred * centred, axis=-1, keepdims=True))
    row_inverse = lax.rsqrt(row_var + EPSILON)
    normed = centred * row_inverse
    return (normed, row_inverse, normed * gain + shift_bias)

def norm_back(grad_normed, gain, normed, row_inverse):
    scaled = grad_normed * gain
    first_mean = lax.optimization_barrier(jnp.mean(scaled, axis=-1, keepdims=True))
    second_mean = lax.optimization_barrier(jnp.mean(scaled * normed, axis=-1, keepdims=True))
    return row_inverse * (scaled - first_mean - normed * second_mean)

def gelu_pair(inputs):
    inner_arg = GELU_C * (inputs + 0.044715 * inputs * inputs * inputs)
    tanh_value = jnp.tanh(inner_arg)
    activated = 0.5 * inputs * (1.0 + tanh_value)
    derivative = 0.5 * (1.0 + tanh_value) + 0.5 * inputs * (1.0 - tanh_value * tanh_value) * GELU_C * (1.0 + 3.0 * 0.044715 * inputs * inputs)
    return (activated, derivative)

def block_scores(query_heads, key_heads, query_pos, key_pos, starts_here):
    scores = jnp.einsum('qhd,khd->hqk', query_heads.astype(jnp.float32), key_heads.astype(jnp.float32)) * HEAD_DIM ** (-0.5)
    visible = (key_pos[None, :] >= starts_here[:, None]) & (key_pos[None, :] <= query_pos[:, None])
    return jnp.where(visible[None], scores, MASKED)

def reference(block_input, ln1_gain, ln1_bias, w_qkv, bias_qv, w_out, bias_out, ln2_gain, ln2_bias, w_fc, bias_fc, w_proj, bias_proj, seq_lengths, out_grad):
    positions = jnp.arange(TOKENS, dtype=jnp.int32)
    seq_ends = jnp.cumsum(seq_lengths).astype(jnp.int32)
    seq_starts = (seq_ends - seq_lengths).astype(jnp.int32)
    token_start = lax.optimization_barrier(jnp.max(jnp.where(seq_starts[None, :] <= positions[:, None], seq_starts[None, :], 0), axis=1)).astype(jnp.int32)
    gain_one = ln1_gain.astype(jnp.float32)
    gain_two = ln2_gain.astype(jnp.float32)
    normed_one, inverse_one, affine_one = layer_norm(block_input, gain_one, ln1_bias.astype(jnp.float32))
    act_one = affine_one.astype(jnp.bfloat16)
    qkv_bias = jnp.concatenate([bias_qv[:D].astype(jnp.float32), jnp.zeros((D,), jnp.float32), bias_qv[D:].astype(jnp.float32)])
    qkv = (jnp.dot(act_one, w_qkv, preferred_element_type=jnp.float32) + qkv_bias).astype(jnp.bfloat16)
    queries = qkv[:, :D]
    key_pad = jnp.concatenate([jnp.zeros((MAXLEN, D), jnp.bfloat16), qkv[:, D:2 * D]], axis=0)
    value_pad = jnp.concatenate([jnp.zeros((MAXLEN, D), jnp.bfloat16), qkv[:, 2 * D:]], axis=0)
    qblock = math.gcd(TOKENS, 512)
    nblocks = TOKENS // qblock
    window = MAXLEN + qblock

    def block_inputs(index):
        begin = (index * qblock).astype(jnp.int32)
        query_heads = lax.dynamic_slice_in_dim(queries, begin, qblock, 0).reshape(qblock, HEADS, HEAD_DIM)
        key_heads = lax.dynamic_slice_in_dim(key_pad, begin, window, 0).reshape(window, HEADS, HEAD_DIM)
        value_heads = lax.dynamic_slice_in_dim(value_pad, begin, window, 0).reshape(window, HEADS, HEAD_DIM)
        query_pos = begin + jnp.arange(qblock, dtype=jnp.int32)
        key_pos = begin - MAXLEN + jnp.arange(window, dtype=jnp.int32)
        starts_here = lax.dynamic_slice_in_dim(token_start, begin, qblock, 0)
        scores = block_scores(query_heads, key_heads, query_pos, key_pos, starts_here)
        return (begin, query_heads, key_heads, value_heads, scores)

    def forward_block(index):
        begin, query_heads, key_heads, value_heads, scores = block_inputs(index)
        row_max = lax.optimization_barrier(jnp.max(scores, axis=-1, keepdims=True))
        total = lax.optimization_barrier(jnp.sum(jnp.exp(scores - row_max), axis=-1, keepdims=True))
        lse = row_max + jnp.log(total)
        attn_probs = jnp.exp(scores - lse).astype(jnp.bfloat16)
        mixed_block = jnp.einsum('hqk,khd->qhd', attn_probs.astype(jnp.float32), value_heads.astype(jnp.float32))
        return (mixed_block.astype(jnp.bfloat16).reshape(qblock, D), lse)
    mixed_blocks, lse_blocks = lax.map(forward_block, jnp.arange(nblocks, dtype=jnp.int32))
    mixed = mixed_blocks.reshape(TOKENS, D)
    hidden_res = block_input + jnp.dot(mixed, w_out, preferred_element_type=jnp.float32) + bias_out.astype(jnp.float32)
    normed_two, inverse_two, affine_two = layer_norm(hidden_res, gain_two, ln2_bias.astype(jnp.float32))
    act_two = affine_two.astype(jnp.bfloat16)
    pre_act = jnp.dot(act_two, w_fc, preferred_element_type=jnp.float32) + bias_fc.astype(jnp.float32)
    activated, derivative = gelu_pair(pre_act)
    gelu_out = activated.astype(jnp.bfloat16)
    block_output = hidden_res + jnp.dot(gelu_out, w_proj, preferred_element_type=jnp.float32) + bias_proj.astype(jnp.float32)
    grad_bias_proj = lax.optimization_barrier(jnp.sum(out_grad, axis=0))
    out_grad_b = out_grad.astype(jnp.bfloat16)
    grad_w_proj = jnp.dot(gelu_out.T, out_grad_b, preferred_element_type=jnp.float32)
    grad_pre = jnp.dot(out_grad_b, w_proj.T, preferred_element_type=jnp.float32) * derivative
    grad_bias_fc = lax.optimization_barrier(jnp.sum(grad_pre, axis=0))
    grad_pre_b = grad_pre.astype(jnp.bfloat16)
    grad_w_fc = jnp.dot(act_two.T, grad_pre_b, preferred_element_type=jnp.float32)
    grad_act_two = jnp.dot(grad_pre_b, w_fc.T, preferred_element_type=jnp.float32)
    grad_ln2_gain = lax.optimization_barrier(jnp.sum(grad_act_two * normed_two, axis=0))
    grad_ln2_bias = lax.optimization_barrier(jnp.sum(grad_act_two, axis=0))
    grad_hidden = out_grad + norm_back(grad_act_two, gain_two, normed_two, inverse_two)
    grad_bias_out = lax.optimization_barrier(jnp.sum(grad_hidden, axis=0))
    grad_hidden_b = grad_hidden.astype(jnp.bfloat16)
    grad_w_out = jnp.dot(mixed.T, grad_hidden_b, preferred_element_type=jnp.float32)
    grad_mixed = jnp.dot(grad_hidden_b, w_out.T, preferred_element_type=jnp.float32).astype(jnp.bfloat16)

    def backward_block(carry, index):
        grad_key_pad, grad_value_pad = carry
        begin, query_heads, key_heads, value_heads, scores = block_inputs(index)
        probs_full = jnp.exp(scores - lse_blocks[index])
        probs_round = probs_full.astype(jnp.bfloat16)
        grad_heads = lax.dynamic_slice_in_dim(grad_mixed, begin, qblock, 0).reshape(qblock, HEADS, HEAD_DIM)
        grad_probs = jnp.einsum('qhd,khd->hqk', grad_heads.astype(jnp.float32), value_heads.astype(jnp.float32))
        row_delta = lax.optimization_barrier(jnp.sum(probs_full * grad_probs, axis=-1, keepdims=True))
        grad_scores = (probs_full * (grad_probs - row_delta) * HEAD_DIM ** (-0.5)).astype(jnp.bfloat16)
        grad_query_block = jnp.einsum('hqk,khd->qhd', grad_scores.astype(jnp.float32), key_heads.astype(jnp.float32)).reshape(qblock, D)
        grad_key_block = jnp.einsum('hqk,qhd->khd', grad_scores.astype(jnp.float32), query_heads.astype(jnp.float32)).reshape(window, D)
        grad_value_block = jnp.einsum('hqk,qhd->khd', probs_round.astype(jnp.float32), grad_heads.astype(jnp.float32)).reshape(window, D)
        grad_key_pad = lax.dynamic_update_slice_in_dim(grad_key_pad, lax.dynamic_slice_in_dim(grad_key_pad, begin, window, 0) + grad_key_block, begin, 0)
        grad_value_pad = lax.dynamic_update_slice_in_dim(grad_value_pad, lax.dynamic_slice_in_dim(grad_value_pad, begin, window, 0) + grad_value_block, begin, 0)
        return ((grad_key_pad, grad_value_pad), grad_query_block)
    empty_pad = jnp.zeros((MAXLEN + TOKENS, D), jnp.float32)
    (grad_key_pad, grad_value_pad), grad_query_blocks = lax.scan(backward_block, (empty_pad, empty_pad), jnp.arange(nblocks, dtype=jnp.int32))
    grad_queries = grad_query_blocks.reshape(TOKENS, D)
    grad_keys = grad_key_pad[MAXLEN:]
    grad_values = grad_value_pad[MAXLEN:]
    grad_bias_qv = jnp.concatenate([lax.optimization_barrier(jnp.sum(grad_queries, axis=0)), lax.optimization_barrier(jnp.sum(grad_values, axis=0))])
    grad_qkv = jnp.concatenate([grad_queries, grad_keys, grad_values], axis=1).astype(jnp.bfloat16)
    grad_w_qkv = jnp.dot(act_one.T, grad_qkv, preferred_element_type=jnp.float32)
    grad_act_one = jnp.dot(grad_qkv, w_qkv.T, preferred_element_type=jnp.float32)
    grad_ln1_gain = lax.optimization_barrier(jnp.sum(grad_act_one * normed_one, axis=0))
    grad_ln1_bias = lax.optimization_barrier(jnp.sum(grad_act_one, axis=0))
    grad_input = grad_hidden + norm_back(grad_act_one, gain_one, normed_one, inverse_one)
    return (block_output, grad_input, grad_ln1_gain, grad_ln1_bias, grad_w_qkv, grad_bias_qv, grad_w_out, grad_bias_out, grad_ln2_gain, grad_ln2_bias, grad_w_fc, grad_bias_fc, grad_w_proj, grad_bias_proj)
```

```python
import math

import jax
import jax.numpy as jnp
from jax import lax
from jax.experimental import pallas as pl
from jax.experimental.pallas import tpu as pltpu
from jax.sharding import PartitionSpec as P

HEADS = 16
HEAD_DIM = 64
REACH = 4
PLANE = 8
INTERPRET = False


EPSILON = 1e-05
GELU_C = math.sqrt(2.0 / math.pi)
MASKED = -1e30


def from_behind(value, axis, steps):
    count = lax.axis_size(axis)
    first, last = (max(0, -steps), min(count, count - steps))
    return lax.ppermute(value, axis, [(source, source + steps) for source in range(first, last)])


def layer_norm(values, gain, shift_bias):
    row_mean = jnp.mean(values, axis=-1, keepdims=True)
    centred = values - row_mean
    row_var = jnp.mean(centred * centred, axis=-1, keepdims=True)
    row_inverse = lax.rsqrt(row_var + EPSILON)
    normed = centred * row_inverse
    return (normed, row_inverse, normed * gain + shift_bias)


def norm_back(grad_normed, gain, normed, row_inverse):
    scaled = grad_normed * gain
    first_mean = jnp.mean(scaled, axis=-1, keepdims=True)
    second_mean = jnp.mean(scaled * normed, axis=-1, keepdims=True)
    return row_inverse * (scaled - first_mean - normed * second_mean)


def gelu_pair(inputs):
    inner_arg = GELU_C * (inputs + 0.044715 * inputs * inputs * inputs)
    tanh_value = jnp.tanh(inner_arg)
    activated = 0.5 * inputs * (1.0 + tanh_value)
    derivative = 0.5 * (1.0 + tanh_value) + 0.5 * inputs * (
        1.0 - tanh_value * tanh_value
    ) * GELU_C * (1.0 + 3.0 * 0.044715 * inputs * inputs)
    return (activated, derivative)


def attention_scores(query_heads, key_heads, query_pos, key_pos, token_start):
    scores = jnp.einsum(
        "qhd,khd->hqk", query_heads, key_heads, preferred_element_type=jnp.float32
    ) * HEAD_DIM ** (-0.5)
    visible = (key_pos[None, :] >= token_start[:, None]) & (key_pos[None, :] <= query_pos[:, None])
    return jnp.where(visible[None], scores, MASKED)


def local_any(
    block_input,
    ln1_gain,
    ln1_bias,
    w_qkv,
    bias_qv,
    w_out,
    bias_out,
    ln2_gain,
    ln2_bias,
    w_fc,
    bias_fc,
    w_proj,
    bias_proj,
    seq_lengths,
    out_grad,
):
    full = (
        lax.all_gather(ln1_gain, "fsdp", axis=0, tiled=True),
        lax.all_gather(ln1_bias, "fsdp", axis=0, tiled=True),
        lax.all_gather(w_qkv, "fsdp", axis=0, tiled=True),
        lax.all_gather(bias_qv, "fsdp", axis=0, tiled=True),
        lax.all_gather(w_out, "fsdp", axis=0, tiled=True),
        lax.all_gather(bias_out, "fsdp", axis=0, tiled=True),
        lax.all_gather(ln2_gain, "fsdp", axis=0, tiled=True),
        lax.all_gather(ln2_bias, "fsdp", axis=0, tiled=True),
        lax.all_gather(w_fc, "fsdp", axis=0, tiled=True),
        lax.all_gather(bias_fc, "fsdp", axis=0, tiled=True),
        lax.all_gather(w_proj, "fsdp", axis=0, tiled=True),
        lax.all_gather(bias_proj, "fsdp", axis=0, tiled=True),
    )
    rows = block_input.shape[0]
    width = block_input.shape[1]
    device = lax.axis_index("fsdp")
    positions = device * rows + jnp.arange(rows, dtype=jnp.int32)
    key_pos = (device - REACH) * rows + jnp.arange((REACH + 1) * rows, dtype=jnp.int32)
    seq_ends = jnp.cumsum(seq_lengths)
    seq_starts = seq_ends - seq_lengths
    token_start = jnp.max(
        jnp.where(seq_starts[None, :] <= positions[:, None], seq_starts[None, :], 0), axis=1
    )
    gain_one = full[0].astype(jnp.float32)
    normed_one, inverse_one, affine_one = layer_norm(
        block_input, gain_one, full[1].astype(jnp.float32)
    )
    act_one = affine_one.astype(jnp.bfloat16)
    qkv_bias = jnp.concatenate(
        [
            full[3][:width].astype(jnp.float32),
            jnp.zeros((width,), jnp.float32),
            full[3][width:].astype(jnp.float32),
        ]
    )
    qkv = (jnp.dot(act_one, full[2], preferred_element_type=jnp.float32) + qkv_bias).astype(
        jnp.bfloat16
    )
    queries = qkv[:, :width]
    kv_own = qkv[:, width:]
    earlier = []
    moving = kv_own
    for distance in range(REACH):
        moving = from_behind(moving, "fsdp", 1)
        earlier.append(moving)
    kv_all = jnp.concatenate(earlier[::-1] + [kv_own], axis=0)
    key_heads = kv_all[:, :width].reshape(-1, HEADS, HEAD_DIM)
    value_heads = kv_all[:, width:].reshape(-1, HEADS, HEAD_DIM)
    query_heads = queries.reshape(rows, HEADS, HEAD_DIM)
    scores = attention_scores(query_heads, key_heads, positions, key_pos, token_start)
    row_max = jnp.max(scores, axis=-1, keepdims=True)
    total = jnp.sum(jnp.exp(scores - row_max), axis=-1, keepdims=True)
    lse = row_max + jnp.log(total)
    attn_probs = jnp.exp(scores - lse).astype(jnp.bfloat16)
    mixed = (
        jnp.einsum("hqk,khd->qhd", attn_probs, value_heads, preferred_element_type=jnp.float32)
        .astype(jnp.bfloat16)
        .reshape(rows, width)
    )
    hidden_res = (
        block_input
        + jnp.dot(mixed, full[4], preferred_element_type=jnp.float32)
        + full[5].astype(jnp.float32)
    )
    gain_two = full[6].astype(jnp.float32)
    normed_two, inverse_two, affine_two = layer_norm(
        hidden_res, gain_two, full[7].astype(jnp.float32)
    )
    act_two = affine_two.astype(jnp.bfloat16)
    pre_act = jnp.dot(act_two, full[8], preferred_element_type=jnp.float32) + full[9].astype(
        jnp.float32
    )
    activated, derivative = gelu_pair(pre_act)
    gelu_out = activated.astype(jnp.bfloat16)
    block_output = (
        hidden_res
        + jnp.dot(gelu_out, full[10], preferred_element_type=jnp.float32)
        + full[11].astype(jnp.float32)
    )
    params_back = (
        lax.all_gather(ln1_gain, "fsdp", axis=0, tiled=True),
        lax.all_gather(ln1_bias, "fsdp", axis=0, tiled=True),
        lax.all_gather(w_qkv, "fsdp", axis=0, tiled=True),
        lax.all_gather(bias_qv, "fsdp", axis=0, tiled=True),
        lax.all_gather(w_out, "fsdp", axis=0, tiled=True),
        lax.all_gather(bias_out, "fsdp", axis=0, tiled=True),
        lax.all_gather(ln2_gain, "fsdp", axis=0, tiled=True),
        lax.all_gather(ln2_bias, "fsdp", axis=0, tiled=True),
        lax.all_gather(w_fc, "fsdp", axis=0, tiled=True),
        lax.all_gather(bias_fc, "fsdp", axis=0, tiled=True),
        lax.all_gather(w_proj, "fsdp", axis=0, tiled=True),
        lax.all_gather(bias_proj, "fsdp", axis=0, tiled=True),
    )
    grad_proj_bias = jnp.sum(out_grad, axis=0)
    out_grad_b = out_grad.astype(jnp.bfloat16)
    grad_proj_weight = jnp.dot(gelu_out.T, out_grad_b, preferred_element_type=jnp.float32)
    grad_pre = (
        jnp.dot(out_grad_b, params_back[10].T, preferred_element_type=jnp.float32) * derivative
    )
    grad_fc_bias = jnp.sum(grad_pre, axis=0)
    grad_pre_b = grad_pre.astype(jnp.bfloat16)
    grad_fc_weight = jnp.dot(act_two.T, grad_pre_b, preferred_element_type=jnp.float32)
    grad_act_two = jnp.dot(grad_pre_b, params_back[8].T, preferred_element_type=jnp.float32)
    grad_ln2_gain = jnp.sum(grad_act_two * normed_two, axis=0)
    grad_ln2_bias = jnp.sum(grad_act_two, axis=0)
    grad_hidden = out_grad + norm_back(
        grad_act_two, params_back[6].astype(jnp.float32), normed_two, inverse_two
    )
    grad_out_bias = jnp.sum(grad_hidden, axis=0)
    grad_hidden_b = grad_hidden.astype(jnp.bfloat16)
    grad_out_weight = jnp.dot(mixed.T, grad_hidden_b, preferred_element_type=jnp.float32)
    grad_mixed = jnp.dot(
        grad_hidden_b, params_back[4].T, preferred_element_type=jnp.float32
    ).astype(jnp.bfloat16)
    grad_heads = grad_mixed.reshape(rows, HEADS, HEAD_DIM)
    scores_again = attention_scores(query_heads, key_heads, positions, key_pos, token_start)
    probs_full = jnp.exp(scores_again - lse)
    probs_round = probs_full.astype(jnp.bfloat16)
    grad_probs = jnp.einsum(
        "qhd,khd->hqk", grad_heads, value_heads, preferred_element_type=jnp.float32
    )
    row_delta = jnp.sum(probs_full * grad_probs, axis=-1, keepdims=True)
    grad_scores = (probs_full * (grad_probs - row_delta) * HEAD_DIM ** (-0.5)).astype(jnp.bfloat16)
    grad_queries = jnp.einsum(
        "hqk,khd->qhd", grad_scores, key_heads, preferred_element_type=jnp.float32
    ).reshape(rows, width)
    grad_keys_all = jnp.einsum(
        "hqk,qhd->khd", grad_scores, query_heads, preferred_element_type=jnp.float32
    ).reshape(-1, width)
    grad_values_all = jnp.einsum(
        "hqk,qhd->khd", probs_round, grad_heads, preferred_element_type=jnp.float32
    ).reshape(-1, width)
    grad_kv_all = jnp.concatenate([grad_keys_all, grad_values_all], axis=1)
    pieces = [
        grad_kv_all[(REACH - distance) * rows : (REACH - distance + 1) * rows]
        for distance in range(REACH + 1)
    ]
    grad_kv = pieces[REACH]
    for distance in range(REACH - 1, -1, -1):
        grad_kv = from_behind(grad_kv, "fsdp", -1) + pieces[distance]
    grad_qv_bias = jnp.concatenate(
        [jnp.sum(grad_queries, axis=0), jnp.sum(grad_kv[:, width:], axis=0)]
    )
    grad_qkv = jnp.concatenate([grad_queries, grad_kv], axis=1).astype(jnp.bfloat16)
    grad_qkv_weight = jnp.dot(act_one.T, grad_qkv, preferred_element_type=jnp.float32)
    grad_act_one = jnp.dot(grad_qkv, params_back[2].T, preferred_element_type=jnp.float32)
    grad_ln1_gain = jnp.sum(grad_act_one * normed_one, axis=0)
    grad_ln1_bias = jnp.sum(grad_act_one, axis=0)
    grad_input = grad_hidden + norm_back(
        grad_act_one, params_back[0].astype(jnp.float32), normed_one, inverse_one
    )
    reduced = tuple(
        (
            lax.psum_scatter(grad_ln1_gain, "fsdp", scatter_dimension=0, tiled=True),
            lax.psum_scatter(grad_ln1_bias, "fsdp", scatter_dimension=0, tiled=True),
            lax.psum_scatter(grad_qkv_weight, "fsdp", scatter_dimension=0, tiled=True),
            lax.psum_scatter(grad_qv_bias, "fsdp", scatter_dimension=0, tiled=True),
            lax.psum_scatter(grad_out_weight, "fsdp", scatter_dimension=0, tiled=True),
            lax.psum_scatter(grad_out_bias, "fsdp", scatter_dimension=0, tiled=True),
            lax.psum_scatter(grad_ln2_gain, "fsdp", scatter_dimension=0, tiled=True),
            lax.psum_scatter(grad_ln2_bias, "fsdp", scatter_dimension=0, tiled=True),
            lax.psum_scatter(grad_fc_weight, "fsdp", scatter_dimension=0, tiled=True),
            lax.psum_scatter(grad_fc_bias, "fsdp", scatter_dimension=0, tiled=True),
            lax.psum_scatter(grad_proj_weight, "fsdp", scatter_dimension=0, tiled=True),
            lax.psum_scatter(grad_proj_bias, "fsdp", scatter_dimension=0, tiled=True),
        )
    )
    return (block_output, grad_input) + reduced


BF = jnp.bfloat16
F32 = jnp.float32
AXIS = "fsdp"


def mm(a, b):
    return jnp.dot(a, b, preferred_element_type=F32)


def mm_nt(a, b):
    return lax.dot_general(a, b, (((1,), (1,)), ((), ())), preferred_element_type=F32)


def mm_tn(a, b):
    return lax.dot_general(a, b, (((0,), (0,)), ((), ())), preferred_element_type=F32)


def pick(array, index):
    return lax.dynamic_index_in_dim(array, index, 0, keepdims=False)


def put(array, block, index):
    return lax.dynamic_update_slice_in_dim(array, block[None], index, 0)


def swap(value, mask):
    count = lax.axis_size(AXIS)
    return lax.ppermute(value, AXIS, [(d, d ^ mask) for d in range(count)])


def spread_vectors(own):
    device = lax.axis_index(AXIS)
    rows = own
    step = 1
    while step < lax.axis_size(AXIS):
        other = swap(rows, step)
        upper = (device & step) != 0
        rows = jnp.where(
            upper, jnp.concatenate([other, rows]), jnp.concatenate([rows, other])
        )
        step *= 2
    return rows


def fold_vectors(terms):
    device = lax.axis_index(AXIS)
    step = lax.axis_size(AXIS) // 2
    while step:
        halves = terms.reshape(2, step, -1)
        bit = (device // step) & 1
        terms = pick(halves, bit) + swap(pick(halves, 1 - bit), step)
        step //= 2
    return terms.reshape(-1)


def plane_gather(value):
    mine = jnp.stack([value, swap(value, 2), swap(value, 4), swap(value, 6)])
    return jnp.concatenate([mine, swap(mine, 1)])


def plane_reduce(partial):
    kept = partial[:4] + swap(partial[4:].astype(BF), 1).astype(F32)
    sent = kept.astype(BF)
    total = kept[0]
    for m in (1, 2, 3):
        total = total + swap(sent[m], 2 * m).astype(F32)
    return total


def plane_exchange(blocks):
    device = lax.axis_index(AXIS)
    core = device & 1
    chip = (device >> 1) & 3
    by_core = blocks.reshape((4, 2) + blocks.shape[1:])
    mine = lax.dynamic_index_in_dim(by_core, core, 1, keepdims=False)
    other = swap(lax.dynamic_index_in_dim(by_core, 1 - core, 1, keepdims=False), 1)
    low = jnp.where(core == 0, mine, other)
    high = jnp.where(core == 0, other, mine)
    pairs = jnp.stack([low, high], 1)
    out = jnp.zeros_like(pairs)
    out = put(out, pick(pairs, chip), chip)
    for m in (1, 2, 3):
        out = put(out, swap(pick(pairs, chip ^ m), 2 * m), chip ^ m)
    return out.reshape(blocks.shape)


def z_gather(value):
    z = lax.axis_index(AXIS) // PLANE
    out = jnp.zeros((4,) + value.shape, value.dtype)
    out = put(out, value, z)
    for m in (1, 2, 3):
        out = put(out, swap(value, PLANE * m), z ^ m)
    return out


def z_reduce(partial):
    z = lax.axis_index(AXIS) // PLANE
    total = pick(partial, z).astype(F32)
    for m in (1, 2, 3):
        total = total + swap(pick(partial, z ^ m).astype(BF), PLANE * m).astype(F32)
    return total


def head_rows_perm(r):
    count = lax.axis_size(AXIS)
    pairs = []
    for d in range(count):
        f = d % PLANE
        pairs.append((d, d - f + 2 * ((f % 4) ^ r) + f // 4))
    return pairs


def key_block(f, u):
    own = u ^ f
    before = (u + 8) ^ f
    own_at = (own >> 1) | ((own & 1) << 2)
    before_at = 8 + ((before & 1) << 1) + ((before >> 1) & 1)
    return jnp.where(u >= 0, own_at, before_at)


def masked_pair(rows):
    lane = lax.broadcasted_iota(jnp.int32, rows.shape, 1)
    zero = jnp.zeros_like(rows)
    first = lane < HEAD_DIM
    return jnp.concatenate([jnp.where(first, rows, zero), jnp.where(first, zero, rows)], 0)


def unpair(both, rows):
    lane = lax.broadcasted_iota(jnp.int32, (rows, both.shape[1]), 1)
    return jnp.where(lane < HEAD_DIM, both[:rows], both[rows:])


def block_probs(f, b, qkv_ref, kv_ref, start_ref):
    rows = qkv_ref.shape[1]
    t = f ^ ((b & 3) * 2 + (b >> 2))
    scaled = (qkv_ref[b, :, 0:128].astype(F32) * HEAD_DIM ** (-0.5)).astype(BF)
    q2 = masked_pair(scaled)
    start = start_ref[b]
    lane = lax.broadcasted_iota(jnp.int32, (rows, 128), 1)
    row = lax.broadcasted_iota(jnp.int32, (rows, 128), 0)
    tiles = []
    places = []
    for j in range(REACH + 1):
        u = t - REACH + j
        at = key_block(f, u)
        places.append(at)
        key_pos = u * 128 + lane
        visible = (key_pos >= start) & (key_pos <= t * 128 + row)
        visible = jnp.concatenate([visible, visible], 0)
        tiles.append(jnp.where(visible, mm_nt(q2, kv_ref[at, :, 0:128]), MASKED))
    scores = jnp.concatenate(tiles, 1)
    top = jnp.max(scores, axis=-1, keepdims=True)
    weights = jnp.exp(scores - top)
    total = jnp.sum(weights, axis=-1, keepdims=True)
    return (places, q2, weights * (1.0 / total))


def attend_kernel(f_ref, qkv_ref, kv_ref, start_ref, out_ref):
    f = f_ref[0]
    rows = qkv_ref.shape[1]

    def body(b, carry):
        places, _, probs = block_probs(f, b, qkv_ref, kv_ref, start_ref)
        probs_b = probs.astype(BF)
        both = jnp.zeros((2 * rows, 128), F32)
        for j, at in enumerate(places):
            both = both + mm(probs_b[:, j * 128 : (j + 1) * 128], kv_ref[at, :, 128:256])
        out_ref[b] = unpair(both, rows).astype(BF)
        return carry

    lax.fori_loop(0, PLANE, body, 0)


def attend_back_kernel(f_ref, qkv_ref, kv_ref, start_ref, grad_ref, dq_ref, dkv_ref):
    f = f_ref[0]
    rows = qkv_ref.shape[1]
    dkv_ref[...] = jnp.zeros_like(dkv_ref)

    def body(b, carry):
        places, q2, probs = block_probs(f, b, qkv_ref, kv_ref, start_ref)
        g2 = masked_pair(grad_ref[b])
        grad_probs = jnp.concatenate(
            [mm_nt(g2, kv_ref[at, :, 128:256]) for at in places], 1
        )
        delta = jnp.sum(probs * grad_probs, axis=-1, keepdims=True)
        grad_scores = (probs * (grad_probs - delta)).astype(BF)
        probs_b = probs.astype(BF)
        both = jnp.zeros((2 * rows, 128), F32)
        for j, at in enumerate(places):
            part = grad_scores[:, j * 128 : (j + 1) * 128]
            both = both + mm(part, kv_ref[at, :, 0:128])
            dkv_ref[at, :, 0:128] += mm_tn(part, q2)
            dkv_ref[at, :, 128:256] += mm_tn(probs_b[:, j * 128 : (j + 1) * 128], g2)
        dq_ref[b] = unpair(both, rows) * HEAD_DIM ** (-0.5)
        return carry

    lax.fori_loop(0, PLANE, body, 0)


def vmem_call(kernel, outs, args):
    return pl.pallas_call(
        kernel,
        out_shape=outs,
        in_specs=[pl.BlockSpec(memory_space=pltpu.SMEM)]
        + [pl.BlockSpec(memory_space=pltpu.VMEM)] * (len(args) - 1),
        out_specs=[pl.BlockSpec(memory_space=pltpu.VMEM)] * len(outs),
        interpret=INTERPRET,
    )(*args)


def local_plane(
    block_input,
    ln1_gain,
    ln1_bias,
    w_qkv,
    bias_qv,
    w_out,
    bias_out,
    ln2_gain,
    ln2_bias,
    w_fc,
    bias_fc,
    w_proj,
    bias_proj,
    seq_lengths,
    out_grad,
):
    count = lax.axis_size(AXIS)
    planes = count // PLANE
    device = lax.axis_index(AXIS)
    z = device // PLANE
    f = device % PLANE
    y = (device >> 2) & 1
    rows, width = block_input.shape
    tokens = PLANE * rows
    share = width // count
    part = width // PLANE
    f_scalar = f.astype(jnp.int32).reshape(1)

    qkv_blocks = w_qkv.reshape(share, 3, PLANE, part).transpose(2, 0, 1, 3)
    w_qkv_here = plane_exchange(qkv_blocks.reshape(PLANE, share, 3 * part))
    w_qkv_all = z_gather(w_qkv_here).reshape(width, 3 * part)

    row_mean = jnp.mean(block_input, axis=-1, keepdims=True)
    centred = block_input - row_mean
    inverse_one = lax.rsqrt(jnp.mean(centred * centred, axis=-1, keepdims=True) + EPSILON)
    normed_one = centred * inverse_one
    normed_all = plane_gather(normed_one.astype(BF)).reshape(tokens, width)

    packed = jnp.concatenate(
        [ln1_gain, ln1_bias, bias_out, ln2_gain, ln2_bias, bias_proj, bias_qv, bias_fc]
    )
    vectors = spread_vectors(packed.reshape(1, -1))

    def whole(i):
        return vectors[:, i * share : (i + 1) * share].reshape(width).astype(F32)

    gain_one, shift_one, b_out, gain_two, shift_two, b_proj = [whole(i) for i in range(6)]
    qv_at = 6 * share
    fc_at = qv_at + bias_qv.shape[0]
    b_qv = vectors[:, qv_at:fc_at].reshape(2, PLANE, part)
    b_qv = lax.dynamic_index_in_dim(b_qv, f, 1, keepdims=False).astype(F32)
    b_fc = vectors[:, fc_at:].reshape(planes, PLANE, -1)
    b_fc = lax.dynamic_index_in_dim(b_fc, f, 1, keepdims=False).reshape(-1).astype(F32)
    b_qkv = jnp.concatenate([b_qv[0], jnp.zeros((part,), F32), b_qv[1]])

    w_out_column = z_gather(w_out)
    w_out_all = jnp.zeros((4,) + w_out.shape, BF)
    for r in range(4):
        arrived = lax.ppermute(pick(w_out_column, (f % 4) ^ r), AXIS, head_rows_perm(r))
        w_out_all = put(w_out_all, arrived, (f // 2) ^ r)
    w_out_all = w_out_all.reshape(part, width)

    fc_blocks = w_fc.reshape(share, planes, PLANE, -1).transpose(2, 0, 1, 3)
    hidden = planes * fc_blocks.shape[3]
    w_fc_here = plane_exchange(fc_blocks.reshape(PLANE, share, hidden))
    w_fc_all = z_gather(w_fc_here).reshape(width, hidden)
    w_proj_all = z_gather(w_proj).reshape(hidden, width)

    act_one = (normed_all.astype(F32) * gain_one + shift_one).astype(BF)
    qkv = (mm(act_one, w_qkv_all) + b_qkv).astype(BF).reshape(PLANE, rows, 3 * part)
    kv_own = qkv[:, :, part:]
    kv_late = lax.dynamic_index_in_dim(
        kv_own.reshape(2, 2, 2, rows, 2 * part), 1 - y, 1, keepdims=False
    ).reshape(4, rows, 2 * part)
    kv_before = from_behind(kv_late, AXIS, PLANE)
    kv_all = jnp.concatenate([kv_own, kv_before])
    block = jnp.arange(PLANE, dtype=jnp.int32)
    order = f ^ ((block & 3) * 2 + (block >> 2))
    positions = (z * tokens + order * rows)[:, None] + jnp.arange(rows, dtype=jnp.int32)[None]
    seq_starts = jnp.cumsum(seq_lengths) - seq_lengths
    token_start = jnp.max(
        jnp.where(seq_starts <= positions[:, :, None], seq_starts, 0), axis=2, keepdims=True
    )
    begins = (token_start - z * tokens).astype(jnp.int32)
    (mixed,) = vmem_call(
        attend_kernel,
        [jax.ShapeDtypeStruct((PLANE, rows, part), BF)],
        (f_scalar, qkv, kv_all, begins),
    )
    mixed = mixed.reshape(tokens, part)
    out_sum = plane_reduce(mm(mixed, w_out_all).reshape(PLANE, rows, width))
    hidden_res = block_input + out_sum + b_out
    normed_two, inverse_two, affine_two = layer_norm(hidden_res, gain_two, shift_two)
    act_two = plane_gather(affine_two.astype(BF)).reshape(tokens, width)
    og = plane_gather(out_grad.astype(BF)).reshape(tokens, width)
    pre_act = mm(act_two, w_fc_all) + b_fc
    activated, derivative = gelu_pair(pre_act)
    gelu_out = activated.astype(BF)

    grad_pre = mm_nt(og, w_proj_all) * derivative
    grad_pre_b = grad_pre.astype(BF)
    grad_act_two = plane_reduce(mm_nt(grad_pre_b, w_fc_all).reshape(PLANE, rows, width))
    grad_hidden = out_grad + norm_back(grad_act_two, gain_two, normed_two, inverse_two)
    grad_hidden_b = plane_gather(grad_hidden.astype(BF)).reshape(tokens, width)
    grad_mixed = mm_nt(grad_hidden_b, w_out_all).astype(BF).reshape(PLANE, rows, part)

    proj_sum = plane_reduce(mm(gelu_out, w_proj_all).reshape(PLANE, rows, width))
    block_output = hidden_res + proj_sum + b_proj
    grad_fc_bias = jnp.sum(grad_pre, axis=0)
    grad_w_proj = z_reduce(mm_tn(gelu_out, og).reshape(planes, -1, width))
    grad_fc = z_reduce(mm_tn(act_two, grad_pre_b).reshape(planes, PLANE * share, hidden))
    grad_fc = plane_exchange(grad_fc.astype(BF).reshape(PLANE, share, hidden))
    grad_w_fc = (
        grad_fc.reshape(PLANE, share, planes, -1).transpose(1, 2, 0, 3).reshape(w_fc.shape)
    ).astype(F32)

    grad_queries, grad_kv_all = vmem_call(
        attend_back_kernel,
        [
            jax.ShapeDtypeStruct((PLANE, rows, part), F32),
            jax.ShapeDtypeStruct((PLANE + 4, rows, 2 * part), F32),
        ],
        (f_scalar, qkv, kv_all, begins, grad_mixed),
    )
    kv_back = from_behind(grad_kv_all[PLANE:].astype(BF), AXIS, -PLANE).astype(F32)
    grad_kv = grad_kv_all[:PLANE].reshape(2, 2, 2, rows, 2 * part)
    late = (jnp.arange(2, dtype=jnp.int32) == 1 - y)[None, :, None, None, None]
    grad_kv = grad_kv + jnp.where(late, kv_back.reshape(2, 1, 2, rows, 2 * part), 0.0)
    grad_kv = grad_kv.reshape(tokens, 2 * part)
    grad_queries = grad_queries.reshape(tokens, part)
    grad_qkv = jnp.concatenate([grad_queries, grad_kv], axis=1)
    qkv_sums = jnp.sum(grad_qkv, axis=0)
    grad_qkv = grad_qkv.astype(BF)
    grad_act_one = plane_reduce(mm_nt(grad_qkv, w_qkv_all).reshape(PLANE, rows, width))
    grad_w = z_reduce(mm_tn(act_one, grad_qkv).reshape(planes, PLANE * share, 3 * part))
    grad_w = plane_exchange(grad_w.astype(BF).reshape(PLANE, share, 3 * part))
    grad_w_qkv = (
        grad_w.reshape(PLANE, share, 3, part).transpose(1, 2, 0, 3).reshape(w_qkv.shape)
    ).astype(F32)

    grad_out_part = mm_tn(mixed, grad_hidden_b).astype(BF).reshape((4,) + w_out.shape)
    grad_out_column = jnp.zeros_like(grad_out_part)
    for r in range(4):
        back = [(target, source) for source, target in head_rows_perm(r)]
        arrived = lax.ppermute(pick(grad_out_part, (f // 2) ^ r), AXIS, back)
        grad_out_column = put(grad_out_column, arrived, (f % 4) ^ r)
    grad_w_out = z_reduce(grad_out_column)

    grad_input = grad_hidden + norm_back(grad_act_one, gain_one, normed_one, inverse_one)

    sums = [
        jnp.sum(grad_act_one * normed_one, axis=0),
        jnp.sum(grad_act_one, axis=0),
        jnp.sum(grad_hidden, axis=0),
        jnp.sum(grad_act_two * normed_two, axis=0),
        jnp.sum(grad_act_two, axis=0),
        jnp.sum(out_grad, axis=0),
    ]
    qv_sums = jnp.stack([qkv_sums[:part], qkv_sums[2 * part :]])
    here = jnp.arange(PLANE, dtype=jnp.int32)[None, :, None] == f
    qv_terms = jnp.where(here, qv_sums[:, None], 0.0).reshape(count, -1)
    fc_terms = jnp.where(here, grad_fc_bias.reshape(planes, 1, -1), 0.0).reshape(count, -1)
    terms = jnp.concatenate([s.reshape(count, share) for s in sums] + [qv_terms, fc_terms], axis=1)
    mine = fold_vectors(terms)
    small = [mine[i * share : (i + 1) * share] for i in range(6)]
    return (
        block_output,
        grad_input,
        small[0],
        small[1],
        grad_w_qkv,
        mine[qv_at:fc_at],
        grad_w_out,
        small[2],
        small[3],
        small[4],
        grad_w_fc,
        mine[fc_at:],
        grad_w_proj,
        small[5],
    )


def solution(mesh):
    return jax.shard_map(
        local_plane if mesh.size == 32 else local_any,
        mesh=mesh,
        in_specs=(
            P("fsdp", None),
            P("fsdp"),
            P("fsdp"),
            P("fsdp", None),
            P("fsdp"),
            P("fsdp", None),
            P("fsdp"),
            P("fsdp"),
            P("fsdp"),
            P("fsdp", None),
            P("fsdp"),
            P("fsdp", None),
            P("fsdp"),
            P(),
            P("fsdp", None),
        ),
        out_specs=(
            P("fsdp", None),
            P("fsdp", None),
            P("fsdp"),
            P("fsdp"),
            P("fsdp", None),
            P("fsdp"),
            P("fsdp", None),
            P("fsdp"),
            P("fsdp"),
            P("fsdp"),
            P("fsdp", None),
            P("fsdp"),
            P("fsdp", None),
            P("fsdp"),
        ),
        check_vma=False,
    )
```

```python
import math

import jax
import jax.numpy as jnp
from jax import lax
from jax.experimental import pallas as pl
from jax.experimental.pallas import tpu as pltpu
from jax.sharding import PartitionSpec as P

HEADS = 16
HEAD_DIM = 64
REACH = 4
PLANE = 8
INTERPRET = False


EPSILON = 1e-05
GELU_C = math.sqrt(2.0 / math.pi)
MASKED = -1e30


def from_behind(value, axis, steps):
    count = lax.axis_size(axis)
    first, last = (max(0, -steps), min(count, count - steps))
    return lax.ppermute(value, axis, [(source, source + steps) for source in range(first, last)])


def layer_norm(values, gain, shift_bias):
    row_mean = jnp.mean(values, axis=-1, keepdims=True)
    centred = values - row_mean
    row_var = jnp.mean(centred * centred, axis=-1, keepdims=True)
    row_inverse = lax.rsqrt(row_var + EPSILON)
    normed = centred * row_inverse
    return (normed, row_inverse, normed * gain + shift_bias)


def norm_back(grad_normed, gain, normed, row_inverse):
    scaled = grad_normed * gain
    first_mean = jnp.mean(scaled, axis=-1, keepdims=True)
    second_mean = jnp.mean(scaled * normed, axis=-1, keepdims=True)
    return row_inverse * (scaled - first_mean - normed * second_mean)


def gelu_pair(inputs):
    inner_arg = GELU_C * (inputs + 0.044715 * inputs * inputs * inputs)
    tanh_value = jnp.tanh(inner_arg)
    activated = 0.5 * inputs * (1.0 + tanh_value)
    derivative = 0.5 * (1.0 + tanh_value) + 0.5 * inputs * (
        1.0 - tanh_value * tanh_value
    ) * GELU_C * (1.0 + 3.0 * 0.044715 * inputs * inputs)
    return (activated, derivative)


def attention_scores(query_heads, key_heads, query_pos, key_pos, token_start):
    scores = jnp.einsum(
        "qhd,khd->hqk", query_heads, key_heads, preferred_element_type=jnp.float32
    ) * HEAD_DIM ** (-0.5)
    visible = (key_pos[None, :] >= token_start[:, None]) & (key_pos[None, :] <= query_pos[:, None])
    return jnp.where(visible[None], scores, MASKED)


def local_any(
    block_input,
    ln1_gain,
    ln1_bias,
    w_qkv,
    bias_qv,
    w_out,
    bias_out,
    ln2_gain,
    ln2_bias,
    w_fc,
    bias_fc,
    w_proj,
    bias_proj,
    seq_lengths,
    out_grad,
):
    full = (
        lax.all_gather(ln1_gain, "fsdp", axis=0, tiled=True),
        lax.all_gather(ln1_bias, "fsdp", axis=0, tiled=True),
        lax.all_gather(w_qkv, "fsdp", axis=0, tiled=True),
        lax.all_gather(bias_qv, "fsdp", axis=0, tiled=True),
        lax.all_gather(w_out, "fsdp", axis=0, tiled=True),
        lax.all_gather(bias_out, "fsdp", axis=0, tiled=True),
        lax.all_gather(ln2_gain, "fsdp", axis=0, tiled=True),
        lax.all_gather(ln2_bias, "fsdp", axis=0, tiled=True),
        lax.all_gather(w_fc, "fsdp", axis=0, tiled=True),
        lax.all_gather(bias_fc, "fsdp", axis=0, tiled=True),
        lax.all_gather(w_proj, "fsdp", axis=0, tiled=True),
        lax.all_gather(bias_proj, "fsdp", axis=0, tiled=True),
    )
    rows = block_input.shape[0]
    width = block_input.shape[1]
    device = lax.axis_index("fsdp")
    positions = device * rows + jnp.arange(rows, dtype=jnp.int32)
    key_pos = (device - REACH) * rows + jnp.arange((REACH + 1) * rows, dtype=jnp.int32)
    seq_ends = jnp.cumsum(seq_lengths)
    seq_starts = seq_ends - seq_lengths
    token_start = jnp.max(
        jnp.where(seq_starts[None, :] <= positions[:, None], seq_starts[None, :], 0), axis=1
    )
    gain_one = full[0].astype(jnp.float32)
    normed_one, inverse_one, affine_one = layer_norm(
        block_input, gain_one, full[1].astype(jnp.float32)
    )
    act_one = affine_one.astype(jnp.bfloat16)
    qkv_bias = jnp.concatenate(
        [
            full[3][:width].astype(jnp.float32),
            jnp.zeros((width,), jnp.float32),
            full[3][width:].astype(jnp.float32),
        ]
    )
    qkv = (jnp.dot(act_one, full[2], preferred_element_type=jnp.float32) + qkv_bias).astype(
        jnp.bfloat16
    )
    queries = qkv[:, :width]
    kv_own = qkv[:, width:]
    earlier = []
    moving = kv_own
    for _ in range(REACH):
        moving = from_behind(moving, "fsdp", 1)
        earlier.append(moving)
    kv_all = jnp.concatenate(earlier[::-1] + [kv_own], axis=0)
    key_heads = kv_all[:, :width].reshape(-1, HEADS, HEAD_DIM)
    value_heads = kv_all[:, width:].reshape(-1, HEADS, HEAD_DIM)
    query_heads = queries.reshape(rows, HEADS, HEAD_DIM)
    scores = attention_scores(query_heads, key_heads, positions, key_pos, token_start)
    row_max = jnp.max(scores, axis=-1, keepdims=True)
    total = jnp.sum(jnp.exp(scores - row_max), axis=-1, keepdims=True)
    lse = row_max + jnp.log(total)
    attn_probs = jnp.exp(scores - lse).astype(jnp.bfloat16)
    mixed = (
        jnp.einsum("hqk,khd->qhd", attn_probs, value_heads, preferred_element_type=jnp.float32)
        .astype(jnp.bfloat16)
        .reshape(rows, width)
    )
    hidden_res = (
        block_input
        + jnp.dot(mixed, full[4], preferred_element_type=jnp.float32)
        + full[5].astype(jnp.float32)
    )
    gain_two = full[6].astype(jnp.float32)
    normed_two, inverse_two, affine_two = layer_norm(
        hidden_res, gain_two, full[7].astype(jnp.float32)
    )
    act_two = affine_two.astype(jnp.bfloat16)
    pre_act = jnp.dot(act_two, full[8], preferred_element_type=jnp.float32) + full[9].astype(
        jnp.float32
    )
    activated, derivative = gelu_pair(pre_act)
    gelu_out = activated.astype(jnp.bfloat16)
    block_output = (
        hidden_res
        + jnp.dot(gelu_out, full[10], preferred_element_type=jnp.float32)
        + full[11].astype(jnp.float32)
    )
    params_back = (
        lax.all_gather(ln1_gain, "fsdp", axis=0, tiled=True),
        lax.all_gather(ln1_bias, "fsdp", axis=0, tiled=True),
        lax.all_gather(w_qkv, "fsdp", axis=0, tiled=True),
        lax.all_gather(bias_qv, "fsdp", axis=0, tiled=True),
        lax.all_gather(w_out, "fsdp", axis=0, tiled=True),
        lax.all_gather(bias_out, "fsdp", axis=0, tiled=True),
        lax.all_gather(ln2_gain, "fsdp", axis=0, tiled=True),
        lax.all_gather(ln2_bias, "fsdp", axis=0, tiled=True),
        lax.all_gather(w_fc, "fsdp", axis=0, tiled=True),
        lax.all_gather(bias_fc, "fsdp", axis=0, tiled=True),
        lax.all_gather(w_proj, "fsdp", axis=0, tiled=True),
        lax.all_gather(bias_proj, "fsdp", axis=0, tiled=True),
    )
    grad_proj_bias = jnp.sum(out_grad, axis=0)
    out_grad_b = out_grad.astype(jnp.bfloat16)
    grad_proj_weight = jnp.dot(gelu_out.T, out_grad_b, preferred_element_type=jnp.float32)
    grad_pre = (
        jnp.dot(out_grad_b, params_back[10].T, preferred_element_type=jnp.float32) * derivative
    )
    grad_fc_bias = jnp.sum(grad_pre, axis=0)
    grad_pre_b = grad_pre.astype(jnp.bfloat16)
    grad_fc_weight = jnp.dot(act_two.T, grad_pre_b, preferred_element_type=jnp.float32)
    grad_act_two = jnp.dot(grad_pre_b, params_back[8].T, preferred_element_type=jnp.float32)
    grad_ln2_gain = jnp.sum(grad_act_two * normed_two, axis=0)
    grad_ln2_bias = jnp.sum(grad_act_two, axis=0)
    grad_hidden = out_grad + norm_back(
        grad_act_two, params_back[6].astype(jnp.float32), normed_two, inverse_two
    )
    grad_out_bias = jnp.sum(grad_hidden, axis=0)
    grad_hidden_b = grad_hidden.astype(jnp.bfloat16)
    grad_out_weight = jnp.dot(mixed.T, grad_hidden_b, preferred_element_type=jnp.float32)
    grad_mixed = jnp.dot(
        grad_hidden_b, params_back[4].T, preferred_element_type=jnp.float32
    ).astype(jnp.bfloat16)
    grad_heads = grad_mixed.reshape(rows, HEADS, HEAD_DIM)
    scores_again = attention_scores(query_heads, key_heads, positions, key_pos, token_start)
    probs_full = jnp.exp(scores_again - lse)
    probs_round = probs_full.astype(jnp.bfloat16)
    grad_probs = jnp.einsum(
        "qhd,khd->hqk", grad_heads, value_heads, preferred_element_type=jnp.float32
    )
    row_delta = jnp.sum(probs_full * grad_probs, axis=-1, keepdims=True)
    grad_scores = (probs_full * (grad_probs - row_delta) * HEAD_DIM ** (-0.5)).astype(jnp.bfloat16)
    grad_queries = jnp.einsum(
        "hqk,khd->qhd", grad_scores, key_heads, preferred_element_type=jnp.float32
    ).reshape(rows, width)
    grad_keys_all = jnp.einsum(
        "hqk,qhd->khd", grad_scores, query_heads, preferred_element_type=jnp.float32
    ).reshape(-1, width)
    grad_values_all = jnp.einsum(
        "hqk,qhd->khd", probs_round, grad_heads, preferred_element_type=jnp.float32
    ).reshape(-1, width)
    grad_kv_all = jnp.concatenate([grad_keys_all, grad_values_all], axis=1)
    pieces = [
        grad_kv_all[(REACH - distance) * rows : (REACH - distance + 1) * rows]
        for distance in range(REACH + 1)
    ]
    grad_kv = pieces[REACH]
    for distance in range(REACH - 1, -1, -1):
        grad_kv = from_behind(grad_kv, "fsdp", -1) + pieces[distance]
    grad_qv_bias = jnp.concatenate(
        [jnp.sum(grad_queries, axis=0), jnp.sum(grad_kv[:, width:], axis=0)]
    )
    grad_qkv = jnp.concatenate([grad_queries, grad_kv], axis=1).astype(jnp.bfloat16)
    grad_qkv_weight = jnp.dot(act_one.T, grad_qkv, preferred_element_type=jnp.float32)
    grad_act_one = jnp.dot(grad_qkv, params_back[2].T, preferred_element_type=jnp.float32)
    grad_ln1_gain = jnp.sum(grad_act_one * normed_one, axis=0)
    grad_ln1_bias = jnp.sum(grad_act_one, axis=0)
    grad_input = grad_hidden + norm_back(
        grad_act_one, params_back[0].astype(jnp.float32), normed_one, inverse_one
    )
    reduced = tuple(
        (
            lax.psum_scatter(grad_ln1_gain, "fsdp", scatter_dimension=0, tiled=True),
            lax.psum_scatter(grad_ln1_bias, "fsdp", scatter_dimension=0, tiled=True),
            lax.psum_scatter(grad_qkv_weight, "fsdp", scatter_dimension=0, tiled=True),
            lax.psum_scatter(grad_qv_bias, "fsdp", scatter_dimension=0, tiled=True),
            lax.psum_scatter(grad_out_weight, "fsdp", scatter_dimension=0, tiled=True),
            lax.psum_scatter(grad_out_bias, "fsdp", scatter_dimension=0, tiled=True),
            lax.psum_scatter(grad_ln2_gain, "fsdp", scatter_dimension=0, tiled=True),
            lax.psum_scatter(grad_ln2_bias, "fsdp", scatter_dimension=0, tiled=True),
            lax.psum_scatter(grad_fc_weight, "fsdp", scatter_dimension=0, tiled=True),
            lax.psum_scatter(grad_fc_bias, "fsdp", scatter_dimension=0, tiled=True),
            lax.psum_scatter(grad_proj_weight, "fsdp", scatter_dimension=0, tiled=True),
            lax.psum_scatter(grad_proj_bias, "fsdp", scatter_dimension=0, tiled=True),
        )
    )
    return (block_output, grad_input) + reduced


BF = jnp.bfloat16
F32 = jnp.float32
AXIS = "fsdp"


def mm(a, b):
    return jnp.dot(a, b, preferred_element_type=F32)


def mm_nt(a, b):
    return lax.dot_general(a, b, (((1,), (1,)), ((), ())), preferred_element_type=F32)


def mm_tn(a, b):
    return lax.dot_general(a, b, (((0,), (0,)), ((), ())), preferred_element_type=F32)


def pick(array, index):
    return lax.dynamic_index_in_dim(array, index, 0, keepdims=False)


def swap(value, mask):
    count = lax.axis_size(AXIS)
    return lax.ppermute(value, AXIS, [(d, d ^ mask) for d in range(count)])


def add_everywhere(terms):
    step = 1
    while step < lax.axis_size(AXIS):
        terms = terms + swap(terms, step)
        step *= 2
    return terms


def chip_groups():
    count = lax.axis_size(AXIS)
    return [
        [first + core + f for f in range(0, PLANE, 2)]
        for first in range(0, count, PLANE)
        for core in (0, 1)
    ]


def over_chips(blocks):
    return lax.all_to_all(blocks, AXIS, 0, 0, axis_index_groups=chip_groups(), tiled=True)


def plane_gather(value):
    mine = over_chips(jnp.broadcast_to(value[None], (PLANE // 2,) + value.shape))
    return (mine, swap(mine, 1))


def halves(rows):
    return [half.reshape(-1, half.shape[-1]) for half in rows]


def core_fold(mine, other):
    arrived = swap(other.astype(BF), 1).astype(F32)
    return (mine + arrived).astype(BF).reshape(PLANE // 2, -1, mine.shape[-1])


def chip_fold(kept):
    return jnp.sum(over_chips(kept).astype(F32), axis=0)


def plane_groups():
    count = lax.axis_size(AXIS)
    return [[first + f for f in range(PLANE)] for first in range(0, count, PLANE)]


def z_groups():
    count = lax.axis_size(AXIS)
    return [[first + f for first in range(0, count, PLANE)] for f in range(PLANE)]


def plane_exchange(blocks):
    return lax.all_to_all(blocks, AXIS, 0, 0, axis_index_groups=plane_groups(), tiled=True)


def z_gather(value):
    return lax.all_gather(value, AXIS, axis_index_groups=z_groups(), axis=0, tiled=True)


def z_reduce(partial):
    return lax.psum_scatter(
        partial.astype(BF), AXIS, axis_index_groups=z_groups(), scatter_dimension=0, tiled=True
    )


def after(value, earlier):
    return lax.optimization_barrier((value, earlier))[0]


def key_block(core, u):
    side = (u & 1) ^ core
    return jnp.where(u >= 0, (u >> 1) + 4 * side, PLANE + ((u + 8) >> 1) - 2 + 2 * side)


def masked_pair(rows):
    lane = lax.broadcasted_iota(jnp.int32, rows.shape, 1)
    zero = jnp.zeros_like(rows)
    first = lane < HEAD_DIM
    return jnp.concatenate([jnp.where(first, rows, zero), jnp.where(first, zero, rows)], 0)


def unpair(both, rows):
    lane = lax.broadcasted_iota(jnp.int32, (rows, both.shape[1]), 1)
    return jnp.where(lane < HEAD_DIM, both[:rows], both[rows:])


def block_probs(core, b, qkv_ref, kv_ref, start_ref):
    rows = qkv_ref.shape[1]
    t = 2 * (b & 3) + (core ^ (b >> 2))
    scaled = (qkv_ref[b, :, 0:128].astype(F32) * HEAD_DIM ** (-0.5)).astype(BF)
    q2 = masked_pair(scaled)
    start = start_ref[b]
    lane = lax.broadcasted_iota(jnp.int32, (rows, 128), 1)
    row = lax.broadcasted_iota(jnp.int32, (rows, 128), 0)
    tiles = []
    places = []
    for j in range(REACH + 1):
        u = t - REACH + j
        at = key_block(core, u)
        places.append(at)
        key_pos = u * 128 + lane
        visible = (key_pos >= start) & (key_pos <= t * 128 + row)
        visible = jnp.concatenate([visible, visible], 0)
        tiles.append(jnp.where(visible, mm_nt(q2, kv_ref[at, :, 0:128]), MASKED))
    scores = jnp.concatenate(tiles, 1)
    top = jnp.max(scores, axis=-1, keepdims=True)
    weights = jnp.exp(scores - top)
    total = jnp.sum(weights, axis=-1, keepdims=True)
    return (places, q2, weights * (1.0 / total))


def attend_kernel(core_ref, qkv_ref, kv_ref, start_ref, out_ref):
    core = core_ref[0]
    rows = qkv_ref.shape[1]

    def body(b, carry):
        places, _, probs = block_probs(core, b, qkv_ref, kv_ref, start_ref)
        probs_b = probs.astype(BF)
        both = jnp.zeros((2 * rows, 128), F32)
        for j, at in enumerate(places):
            both = both + mm(probs_b[:, j * 128 : (j + 1) * 128], kv_ref[at, :, 128:256])
        out_ref[b] = unpair(both, rows).astype(BF)
        return carry

    lax.fori_loop(0, PLANE, body, 0)


def attend_back_kernel(core_ref, qkv_ref, kv_ref, start_ref, grad_ref, dq_ref, dkv_ref):
    core = core_ref[0]
    rows = qkv_ref.shape[1]
    dkv_ref[...] = jnp.zeros_like(dkv_ref)

    def body(b, carry):
        places, q2, probs = block_probs(core, b, qkv_ref, kv_ref, start_ref)
        g2 = masked_pair(grad_ref[b])
        grad_probs = jnp.concatenate(
            [mm_nt(g2, kv_ref[at, :, 128:256]) for at in places], 1
        )
        delta = jnp.sum(probs * grad_probs, axis=-1, keepdims=True)
        grad_scores = (probs * (grad_probs - delta)).astype(BF)
        probs_b = probs.astype(BF)
        both = jnp.zeros((2 * rows, 128), F32)
        for j, at in enumerate(places):
            part = grad_scores[:, j * 128 : (j + 1) * 128]
            both = both + mm(part, kv_ref[at, :, 0:128])
            dkv_ref[at, :, 0:128] += mm_tn(part, q2)
            dkv_ref[at, :, 128:256] += mm_tn(probs_b[:, j * 128 : (j + 1) * 128], g2)
        dq_ref[b] = unpair(both, rows) * HEAD_DIM ** (-0.5)
        return carry

    lax.fori_loop(0, PLANE, body, 0)


def vmem_call(kernel, outs, args):
    return pl.pallas_call(
        kernel,
        out_shape=outs,
        in_specs=[pl.BlockSpec(memory_space=pltpu.SMEM)]
        + [pl.BlockSpec(memory_space=pltpu.VMEM)] * (len(args) - 1),
        out_specs=[pl.BlockSpec(memory_space=pltpu.VMEM)] * len(outs),
        interpret=INTERPRET,
    )(*args)


def local_plane(
    block_input,
    ln1_gain,
    ln1_bias,
    w_qkv,
    bias_qv,
    w_out,
    bias_out,
    ln2_gain,
    ln2_bias,
    w_fc,
    bias_fc,
    w_proj,
    bias_proj,
    seq_lengths,
    out_grad,
):
    count = lax.axis_size(AXIS)
    planes = count // PLANE
    device = lax.axis_index(AXIS)
    z = device // PLANE
    f = device % PLANE
    core = device & 1
    rows, width = block_input.shape
    tokens = PLANE * rows
    share = width // count
    part = width // PLANE
    core_scalar = core.astype(jnp.int32).reshape(1)

    vectors = [ln1_gain, ln1_bias, bias_out, ln2_gain, ln2_bias, bias_proj, bias_qv, bias_fc]
    packed = jnp.concatenate([vector.astype(F32) for vector in vectors]).astype(BF)
    lanes = packed.shape[0]
    qkv_blocks = w_qkv.reshape(share, 3, PLANE, part).transpose(2, 0, 1, 3)
    fc_blocks = w_fc.reshape(share, planes, PLANE, -1).transpose(2, 0, 1, 3)
    hidden = planes * fc_blocks.shape[3]
    slices = jnp.concatenate(
        [
            qkv_blocks.reshape(PLANE, share, 3 * part),
            fc_blocks.reshape(PLANE, share, hidden),
        ],
        axis=2,
    )
    extra = jnp.pad(packed.reshape(1, 1, lanes), ((0, 0), (0, 7), (0, slices.shape[2] - lanes)))
    extra = jnp.broadcast_to(extra, (PLANE, 8, slices.shape[2]))
    arrived = plane_exchange(jnp.concatenate([slices, extra], axis=1))

    row_mean = jnp.mean(block_input, axis=-1, keepdims=True)
    centred = block_input - row_mean
    inverse_one = lax.rsqrt(jnp.mean(centred * centred, axis=-1, keepdims=True) + EPSILON)
    normed_one = centred * inverse_one
    normed_all = plane_gather(normed_one.astype(BF))

    first = z_gather(arrived[:, :, : 3 * part].reshape(-1, 3 * part))
    first = first.reshape(count, share + 8, 3 * part)
    w_qkv_all = first[:, :share].reshape(width, 3 * part)
    vectors = first[:, share, :lanes]

    w_out_column = z_gather(w_out).reshape(planes, share, width)
    og_all = lax.all_gather(
        after(out_grad.astype(BF), w_qkv_all),
        AXIS,
        axis_index_groups=plane_groups(),
        axis=0,
        tiled=True,
    ).reshape(PLANE // 2, 2, rows, width)
    w_fc_here = arrived[:, :share, 3 * part :].reshape(PLANE * share, hidden)
    w_fc_all = z_gather(after(w_fc_here, w_qkv_all))

    def whole(i):
        return vectors[:, i * share : (i + 1) * share].reshape(width).astype(F32)

    gain_one, shift_one, b_out, gain_two, shift_two, b_proj = [whole(i) for i in range(6)]
    qv_at = 6 * share
    fc_at = qv_at + bias_qv.shape[0]
    b_qv = vectors[:, qv_at:fc_at].reshape(2, PLANE, part)
    b_qv = lax.dynamic_index_in_dim(b_qv, f, 1, keepdims=False).astype(F32)
    b_fc = vectors[:, fc_at:].reshape(planes, PLANE, -1)
    b_fc = lax.dynamic_index_in_dim(b_fc, f, 1, keepdims=False).reshape(-1).astype(F32)
    b_qkv = jnp.concatenate([b_qv[0], jnp.zeros((part,), F32), b_qv[1]])

    act_one = [
        (half.astype(F32) * gain_one + shift_one).astype(BF) for half in halves(normed_all)
    ]
    qkv = jnp.concatenate([(mm(half, w_qkv_all) + b_qkv).astype(BF) for half in act_one])
    qkv = qkv.reshape(PLANE, rows, 3 * part)
    kv_own = qkv[:, :, part:]
    kv_late = kv_own.reshape(2, 4, rows, 2 * part)[:, 2:].reshape(4, rows, 2 * part)
    kv_before = from_behind(kv_late, AXIS, PLANE)
    kv_all = jnp.concatenate([kv_own, kv_before])
    block = jnp.arange(PLANE, dtype=jnp.int32)
    order = 2 * (block & 3) + (core ^ (block >> 2))
    positions = (z * tokens + order * rows)[:, None] + jnp.arange(rows, dtype=jnp.int32)[None]
    seq_starts = jnp.cumsum(seq_lengths) - seq_lengths
    token_start = jnp.max(
        jnp.where(seq_starts <= positions[:, :, None], seq_starts, 0), axis=2, keepdims=True
    )
    begins = (token_start - z * tokens).astype(jnp.int32)
    w_proj_all = z_gather(after(w_proj, qkv))
    w_out_column = after(w_out_column, qkv)
    w_out_all = plane_exchange(jnp.repeat(w_out_column, 2, axis=0))
    w_out_all = lax.dynamic_slice_in_dim(w_out_all, 4 * core, 4, 0).reshape(part, width)
    (mixed,) = vmem_call(
        attend_kernel,
        [jax.ShapeDtypeStruct((PLANE, rows, part), BF)],
        (core_scalar, qkv, kv_all, begins),
    )
    mixed = halves((mixed[:4], mixed[4:]))
    out_sum = chip_fold(core_fold(*[mm(half, w_out_all) for half in mixed]))
    hidden_res = block_input + out_sum + b_out
    normed_two, inverse_two, affine_two = layer_norm(hidden_res, gain_two, shift_two)
    act_two = halves(plane_gather(affine_two.astype(BF)))
    og = [
        lax.dynamic_index_in_dim(og_all, side, 1, keepdims=False).reshape(-1, width)
        for side in (core, 1 - core)
    ]
    pairs = [gelu_pair(mm(half, w_fc_all) + b_fc) for half in act_two]
    gelu_out = [activated.astype(BF) for activated, _ in pairs]

    grad_pre = [mm_nt(half, w_proj_all) * pair[1] for half, pair in zip(og, pairs)]
    grad_pre_b = [half.astype(BF) for half in grad_pre]
    partial_two = [mm_nt(half, w_fc_all) for half in grad_pre_b]
    gelu_late, pre_late, act_late, partial_two = lax.optimization_barrier(
        (gelu_out, grad_pre_b, act_two, partial_two)
    )
    kept_two = core_fold(*partial_two)
    grad_act_two = chip_fold(kept_two)
    fc_part = (mm_tn(act_late[0], pre_late[0]) + mm_tn(act_late[1], pre_late[1])).astype(BF)
    proj_part = (mm_tn(gelu_late[0], og[0]) + mm_tn(gelu_late[1], og[1])).astype(BF)
    grad_w_fc_here = z_reduce(fc_part)
    grad_w_proj = z_reduce(proj_part).astype(F32)
    proj_terms = [mm(half, w_proj_all) for half in gelu_late]
    kept_proj = core_fold(*proj_terms)
    grad_fc_bias = jnp.sum(grad_pre[0], axis=0) + jnp.sum(grad_pre[1], axis=0)
    grad_hidden = out_grad + norm_back(grad_act_two, gain_two, normed_two, inverse_two)
    grad_hidden_b = halves(plane_gather(grad_hidden.astype(BF)))
    grad_mixed = jnp.concatenate([mm_nt(half, w_out_all).astype(BF) for half in grad_hidden_b])
    grad_mixed, fc_part, proj_part, kept_proj = lax.optimization_barrier(
        (grad_mixed, fc_part, proj_part, kept_proj)
    )
    grad_mixed = grad_mixed.reshape(PLANE, rows, part)
    proj_sum = chip_fold(kept_proj)
    block_output = hidden_res + proj_sum + b_proj

    grad_queries, grad_kv_all = vmem_call(
        attend_back_kernel,
        [
            jax.ShapeDtypeStruct((PLANE, rows, part), F32),
            jax.ShapeDtypeStruct((PLANE + 4, rows, 2 * part), F32),
        ],
        (core_scalar, qkv, kv_all, begins, grad_mixed),
    )
    kv_back = from_behind(grad_kv_all[PLANE:].astype(BF), AXIS, -PLANE).astype(F32)
    grad_kv = grad_kv_all[:PLANE].reshape(2, 4, rows, 2 * part)
    kv_back = jnp.pad(kv_back.reshape(2, 2, rows, 2 * part), ((0, 0), (2, 0), (0, 0), (0, 0)))
    grad_kv = (grad_kv + kv_back).reshape(tokens, 2 * part)
    grad_queries = grad_queries.reshape(tokens, part)
    grad_qkv = jnp.concatenate([grad_queries, grad_kv], axis=1)
    qkv_sums = jnp.sum(grad_qkv, axis=0)
    grad_qkv = grad_qkv.astype(BF)
    grad_qkv = [grad_qkv[: tokens // 2], grad_qkv[tokens // 2 :]]
    qkv_part = (mm_tn(act_one[0], grad_qkv[0]) + mm_tn(act_one[1], grad_qkv[1])).astype(BF)
    grad_w_qkv_here = z_reduce(qkv_part)
    grad_qkv = after(grad_qkv, qkv_part)
    partial_one = [mm_nt(half, w_qkv_all) for half in grad_qkv]
    kept_one = core_fold(*partial_one)
    grad_act_one = chip_fold(kept_one)

    mixed = after(mixed, grad_queries)
    out_part = mm_tn(mixed[0], grad_hidden_b[0]) + mm_tn(mixed[1], grad_hidden_b[1])
    out_part = jnp.tile(out_part.astype(BF).reshape((4,) + w_out.shape), (2, 1, 1))
    out_part = plane_exchange(out_part).reshape((4, 2) + w_out.shape)
    out_part = lax.dynamic_index_in_dim(out_part, f // 4, 1, keepdims=False)
    grad_w_out = z_reduce(out_part.reshape(width // PLANE, width))

    leaving = jnp.concatenate([grad_w_qkv_here, grad_w_fc_here], axis=1)
    landed = plane_exchange(leaving.reshape(PLANE, share, 3 * part + hidden))
    grad_w_out = after(grad_w_out, landed).astype(F32)
    landed = landed.astype(F32)
    grad_w_qkv = landed[:, :, : 3 * part].reshape(PLANE, share, 3, part)
    grad_w_qkv = grad_w_qkv.transpose(1, 2, 0, 3).reshape(w_qkv.shape)
    grad_w_fc = landed[:, :, 3 * part :].reshape(PLANE, share, planes, -1)
    grad_w_fc = grad_w_fc.transpose(1, 2, 0, 3).reshape(w_fc.shape)

    grad_input = grad_hidden + norm_back(grad_act_one, gain_one, normed_one, inverse_one)

    normed_halves = [half.astype(F32) for half in halves(normed_all)]
    sums = [
        jnp.sum(partial_one[0] * normed_halves[0], axis=0)
        + jnp.sum(partial_one[1] * normed_halves[1], axis=0),
        jnp.sum(partial_one[0], axis=0) + jnp.sum(partial_one[1], axis=0),
        jnp.sum(grad_hidden, axis=0),
        jnp.sum(grad_act_two * normed_two, axis=0),
        jnp.sum(grad_act_two, axis=0),
        jnp.sum(out_grad, axis=0),
    ]
    qv_sums = jnp.stack([qkv_sums[:part], qkv_sums[2 * part :]])
    here = (jnp.arange(width, dtype=jnp.int32) // part == f)[None]
    qv_terms = jnp.where(here, jnp.tile(qv_sums, (1, PLANE)), 0.0)
    fc_terms = jnp.where(here, jnp.tile(grad_fc_bias.reshape(planes, part), (1, PLANE)), 0.0)
    terms = jnp.concatenate([jnp.stack(sums), qv_terms, fc_terms])
    total = add_everywhere(terms)
    small = pick(total[:6].reshape(6, count, share).transpose(1, 0, 2), device)
    small_qv = pick(total[6:8].reshape(count, -1), device)
    small_fc = pick(total[8:].reshape(count, -1), device)
    return (
        block_output,
        grad_input,
        small[0],
        small[1],
        grad_w_qkv,
        small_qv,
        grad_w_out,
        small[2],
        small[3],
        small[4],
        grad_w_fc,
        small_fc,
        grad_w_proj,
        small[5],
    )


def solution(mesh):
    if mesh.size != 32:
        return planned(mesh, local_any)
    return planned(mesh, local_plane)


def planned(mesh, local):
    return jax.shard_map(
        local,
        mesh=mesh,
        in_specs=(
            P("fsdp", None),
            P("fsdp"),
            P("fsdp"),
            P("fsdp", None),
            P("fsdp"),
            P("fsdp", None),
            P("fsdp"),
            P("fsdp"),
            P("fsdp"),
            P("fsdp", None),
            P("fsdp"),
            P("fsdp", None),
            P("fsdp"),
            P(),
            P("fsdp", None),
        ),
        out_specs=(
            P("fsdp", None),
            P("fsdp", None),
            P("fsdp"),
            P("fsdp"),
            P("fsdp", None),
            P("fsdp"),
            P("fsdp", None),
            P("fsdp"),
            P("fsdp"),
            P("fsdp"),
            P("fsdp", None),
            P("fsdp"),
            P("fsdp", None),
            P("fsdp"),
        ),
        check_vma=False,
    )
```

```python
import math

import jax
import jax.numpy as jnp
from jax import lax
from jax.experimental import pallas as pl
from jax.experimental.pallas import tpu as pltpu
from jax.sharding import PartitionSpec as P

HEADS = 16
HEAD_DIM = 64
REACH = 4
PLANE = 8
INTERPRET = False
AXIS = "fsdp"


EPSILON = 1e-05
GELU_C = math.sqrt(2.0 / math.pi)
MASKED = -1e30


def from_behind(value, axis, steps):
    count = lax.axis_size(axis)
    first, last = (max(0, -steps), min(count, count - steps))
    return lax.ppermute(value, axis, [(source, source + steps) for source in range(first, last)])


def layer_norm(values, gain, shift_bias):
    row_mean = jnp.mean(values, axis=-1, keepdims=True)
    centred = values - row_mean
    row_var = jnp.mean(centred * centred, axis=-1, keepdims=True)
    row_inverse = lax.rsqrt(row_var + EPSILON)
    normed = centred * row_inverse
    return (normed, row_inverse, normed * gain + shift_bias)


def norm_back(grad_normed, gain, normed, row_inverse):
    scaled = grad_normed * gain
    first_mean = jnp.mean(scaled, axis=-1, keepdims=True)
    second_mean = jnp.mean(scaled * normed, axis=-1, keepdims=True)
    return row_inverse * (scaled - first_mean - normed * second_mean)


def gelu_pair(inputs):
    inner_arg = GELU_C * (inputs + 0.044715 * inputs * inputs * inputs)
    tanh_value = jnp.tanh(inner_arg)
    activated = 0.5 * inputs * (1.0 + tanh_value)
    derivative = 0.5 * (1.0 + tanh_value) + 0.5 * inputs * (
        1.0 - tanh_value * tanh_value
    ) * GELU_C * (1.0 + 3.0 * 0.044715 * inputs * inputs)
    return (activated, derivative)


def attention_scores(query_heads, key_heads, query_pos, key_pos, token_start):
    scores = jnp.einsum(
        "qhd,khd->hqk", query_heads, key_heads, preferred_element_type=jnp.float32
    ) * HEAD_DIM ** (-0.5)
    visible = (key_pos[None, :] >= token_start[:, None]) & (key_pos[None, :] <= query_pos[:, None])
    return jnp.where(visible[None], scores, MASKED)


def local_any(
    block_input,
    ln1_gain,
    ln1_bias,
    w_qkv,
    bias_qv,
    w_out,
    bias_out,
    ln2_gain,
    ln2_bias,
    w_fc,
    bias_fc,
    w_proj,
    bias_proj,
    seq_lengths,
    out_grad,
):
    full = (
        lax.all_gather(ln1_gain, AXIS, axis=0, tiled=True),
        lax.all_gather(ln1_bias, AXIS, axis=0, tiled=True),
        lax.all_gather(w_qkv, AXIS, axis=0, tiled=True),
        lax.all_gather(bias_qv, AXIS, axis=0, tiled=True),
        lax.all_gather(w_out, AXIS, axis=0, tiled=True),
        lax.all_gather(bias_out, AXIS, axis=0, tiled=True),
        lax.all_gather(ln2_gain, AXIS, axis=0, tiled=True),
        lax.all_gather(ln2_bias, AXIS, axis=0, tiled=True),
        lax.all_gather(w_fc, AXIS, axis=0, tiled=True),
        lax.all_gather(bias_fc, AXIS, axis=0, tiled=True),
        lax.all_gather(w_proj, AXIS, axis=0, tiled=True),
        lax.all_gather(bias_proj, AXIS, axis=0, tiled=True),
    )
    rows = block_input.shape[0]
    width = block_input.shape[1]
    device = lax.axis_index(AXIS)
    positions = device * rows + jnp.arange(rows, dtype=jnp.int32)
    key_pos = (device - REACH) * rows + jnp.arange((REACH + 1) * rows, dtype=jnp.int32)
    seq_ends = jnp.cumsum(seq_lengths)
    seq_starts = seq_ends - seq_lengths
    token_start = jnp.max(
        jnp.where(seq_starts[None, :] <= positions[:, None], seq_starts[None, :], 0), axis=1
    )
    gain_one = full[0].astype(jnp.float32)
    normed_one, inverse_one, affine_one = layer_norm(
        block_input, gain_one, full[1].astype(jnp.float32)
    )
    act_one = affine_one.astype(jnp.bfloat16)
    qkv_bias = jnp.concatenate(
        [
            full[3][:width].astype(jnp.float32),
            jnp.zeros((width,), jnp.float32),
            full[3][width:].astype(jnp.float32),
        ]
    )
    qkv = (jnp.dot(act_one, full[2], preferred_element_type=jnp.float32) + qkv_bias).astype(
        jnp.bfloat16
    )
    queries = qkv[:, :width]
    kv_own = qkv[:, width:]
    earlier = []
    moving = kv_own
    for _ in range(REACH):
        moving = from_behind(moving, AXIS, 1)
        earlier.append(moving)
    kv_all = jnp.concatenate(earlier[::-1] + [kv_own], axis=0)
    key_heads = kv_all[:, :width].reshape(-1, HEADS, HEAD_DIM)
    value_heads = kv_all[:, width:].reshape(-1, HEADS, HEAD_DIM)
    query_heads = queries.reshape(rows, HEADS, HEAD_DIM)
    scores = attention_scores(query_heads, key_heads, positions, key_pos, token_start)
    row_max = jnp.max(scores, axis=-1, keepdims=True)
    total = jnp.sum(jnp.exp(scores - row_max), axis=-1, keepdims=True)
    lse = row_max + jnp.log(total)
    attn_probs = jnp.exp(scores - lse).astype(jnp.bfloat16)
    mixed = (
        jnp.einsum("hqk,khd->qhd", attn_probs, value_heads, preferred_element_type=jnp.float32)
        .astype(jnp.bfloat16)
        .reshape(rows, width)
    )
    hidden_res = (
        block_input
        + jnp.dot(mixed, full[4], preferred_element_type=jnp.float32)
        + full[5].astype(jnp.float32)
    )
    gain_two = full[6].astype(jnp.float32)
    normed_two, inverse_two, affine_two = layer_norm(
        hidden_res, gain_two, full[7].astype(jnp.float32)
    )
    act_two = affine_two.astype(jnp.bfloat16)
    pre_act = jnp.dot(act_two, full[8], preferred_element_type=jnp.float32) + full[9].astype(
        jnp.float32
    )
    activated, derivative = gelu_pair(pre_act)
    gelu_out = activated.astype(jnp.bfloat16)
    block_output = (
        hidden_res
        + jnp.dot(gelu_out, full[10], preferred_element_type=jnp.float32)
        + full[11].astype(jnp.float32)
    )
    params_back = (
        lax.all_gather(ln1_gain, AXIS, axis=0, tiled=True),
        lax.all_gather(ln1_bias, AXIS, axis=0, tiled=True),
        lax.all_gather(w_qkv, AXIS, axis=0, tiled=True),
        lax.all_gather(bias_qv, AXIS, axis=0, tiled=True),
        lax.all_gather(w_out, AXIS, axis=0, tiled=True),
        lax.all_gather(bias_out, AXIS, axis=0, tiled=True),
        lax.all_gather(ln2_gain, AXIS, axis=0, tiled=True),
        lax.all_gather(ln2_bias, AXIS, axis=0, tiled=True),
        lax.all_gather(w_fc, AXIS, axis=0, tiled=True),
        lax.all_gather(bias_fc, AXIS, axis=0, tiled=True),
        lax.all_gather(w_proj, AXIS, axis=0, tiled=True),
        lax.all_gather(bias_proj, AXIS, axis=0, tiled=True),
    )
    grad_proj_bias = jnp.sum(out_grad, axis=0)
    out_grad_b = out_grad.astype(jnp.bfloat16)
    grad_proj_weight = jnp.dot(gelu_out.T, out_grad_b, preferred_element_type=jnp.float32)
    grad_pre = (
        jnp.dot(out_grad_b, params_back[10].T, preferred_element_type=jnp.float32) * derivative
    )
    grad_fc_bias = jnp.sum(grad_pre, axis=0)
    grad_pre_b = grad_pre.astype(jnp.bfloat16)
    grad_fc_weight = jnp.dot(act_two.T, grad_pre_b, preferred_element_type=jnp.float32)
    grad_act_two = jnp.dot(grad_pre_b, params_back[8].T, preferred_element_type=jnp.float32)
    grad_ln2_gain = jnp.sum(grad_act_two * normed_two, axis=0)
    grad_ln2_bias = jnp.sum(grad_act_two, axis=0)
    grad_hidden = out_grad + norm_back(
        grad_act_two, params_back[6].astype(jnp.float32), normed_two, inverse_two
    )
    grad_out_bias = jnp.sum(grad_hidden, axis=0)
    grad_hidden_b = grad_hidden.astype(jnp.bfloat16)
    grad_out_weight = jnp.dot(mixed.T, grad_hidden_b, preferred_element_type=jnp.float32)
    grad_mixed = jnp.dot(
        grad_hidden_b, params_back[4].T, preferred_element_type=jnp.float32
    ).astype(jnp.bfloat16)
    grad_heads = grad_mixed.reshape(rows, HEADS, HEAD_DIM)
    scores_again = attention_scores(query_heads, key_heads, positions, key_pos, token_start)
    probs_full = jnp.exp(scores_again - lse)
    probs_round = probs_full.astype(jnp.bfloat16)
    grad_probs = jnp.einsum(
        "qhd,khd->hqk", grad_heads, value_heads, preferred_element_type=jnp.float32
    )
    row_delta = jnp.sum(probs_full * grad_probs, axis=-1, keepdims=True)
    grad_scores = (probs_full * (grad_probs - row_delta) * HEAD_DIM ** (-0.5)).astype(jnp.bfloat16)
    grad_queries = jnp.einsum(
        "hqk,khd->qhd", grad_scores, key_heads, preferred_element_type=jnp.float32
    ).reshape(rows, width)
    grad_keys_all = jnp.einsum(
        "hqk,qhd->khd", grad_scores, query_heads, preferred_element_type=jnp.float32
    ).reshape(-1, width)
    grad_values_all = jnp.einsum(
        "hqk,qhd->khd", probs_round, grad_heads, preferred_element_type=jnp.float32
    ).reshape(-1, width)
    grad_kv_all = jnp.concatenate([grad_keys_all, grad_values_all], axis=1)
    pieces = [
        grad_kv_all[(REACH - distance) * rows : (REACH - distance + 1) * rows]
        for distance in range(REACH + 1)
    ]
    grad_kv = pieces[REACH]
    for distance in range(REACH - 1, -1, -1):
        grad_kv = from_behind(grad_kv, AXIS, -1) + pieces[distance]
    grad_qv_bias = jnp.concatenate(
        [jnp.sum(grad_queries, axis=0), jnp.sum(grad_kv[:, width:], axis=0)]
    )
    grad_qkv = jnp.concatenate([grad_queries, grad_kv], axis=1).astype(jnp.bfloat16)
    grad_qkv_weight = jnp.dot(act_one.T, grad_qkv, preferred_element_type=jnp.float32)
    grad_act_one = jnp.dot(grad_qkv, params_back[2].T, preferred_element_type=jnp.float32)
    grad_ln1_gain = jnp.sum(grad_act_one * normed_one, axis=0)
    grad_ln1_bias = jnp.sum(grad_act_one, axis=0)
    grad_input = grad_hidden + norm_back(
        grad_act_one, params_back[0].astype(jnp.float32), normed_one, inverse_one
    )
    reduced = tuple(
        (
            lax.psum_scatter(grad_ln1_gain, AXIS, scatter_dimension=0, tiled=True),
            lax.psum_scatter(grad_ln1_bias, AXIS, scatter_dimension=0, tiled=True),
            lax.psum_scatter(grad_qkv_weight, AXIS, scatter_dimension=0, tiled=True),
            lax.psum_scatter(grad_qv_bias, AXIS, scatter_dimension=0, tiled=True),
            lax.psum_scatter(grad_out_weight, AXIS, scatter_dimension=0, tiled=True),
            lax.psum_scatter(grad_out_bias, AXIS, scatter_dimension=0, tiled=True),
            lax.psum_scatter(grad_ln2_gain, AXIS, scatter_dimension=0, tiled=True),
            lax.psum_scatter(grad_ln2_bias, AXIS, scatter_dimension=0, tiled=True),
            lax.psum_scatter(grad_fc_weight, AXIS, scatter_dimension=0, tiled=True),
            lax.psum_scatter(grad_fc_bias, AXIS, scatter_dimension=0, tiled=True),
            lax.psum_scatter(grad_proj_weight, AXIS, scatter_dimension=0, tiled=True),
            lax.psum_scatter(grad_proj_bias, AXIS, scatter_dimension=0, tiled=True),
        )
    )
    return (block_output, grad_input) + reduced


BF = jnp.bfloat16
F32 = jnp.float32


def mm(a, b):
    return jnp.dot(a, b, preferred_element_type=F32)


def mm_nt(a, b):
    return lax.dot_general(a, b, (((1,), (1,)), ((), ())), preferred_element_type=F32)


def mm_tn(a, b):
    return lax.dot_general(a, b, (((0,), (0,)), ((), ())), preferred_element_type=F32)


def pick(array, index):
    return lax.dynamic_index_in_dim(array, index, 0, keepdims=False)


def swap(value, mask):
    count = lax.axis_size(AXIS)
    return lax.ppermute(value, AXIS, [(d, d ^ mask) for d in range(count)])


def add_everywhere(terms):
    step = 1
    while step < lax.axis_size(AXIS):
        terms = terms + swap(terms, step)
        step *= 2
    return terms


def chip_groups():
    count = lax.axis_size(AXIS)
    return [
        [first + core + f for f in range(0, PLANE, 2)]
        for first in range(0, count, PLANE)
        for core in (0, 1)
    ]


def over_chips(blocks):
    return lax.all_to_all(blocks, AXIS, 0, 0, axis_index_groups=chip_groups(), tiled=True)


def plane_gather(value):
    mine = over_chips(jnp.broadcast_to(value[None], (PLANE // 2,) + value.shape))
    return (mine, swap(mine, 1))


def halves(rows):
    return [half.reshape(-1, half.shape[-1]) for half in rows]


def core_fold(mine, other):
    arrived = swap(other.astype(BF), 1).astype(F32)
    return (mine + arrived).astype(BF).reshape(PLANE // 2, -1, mine.shape[-1])


def chip_fold(kept):
    return jnp.sum(over_chips(kept).astype(F32), axis=0)


def plane_groups():
    count = lax.axis_size(AXIS)
    return [[first + f for f in range(PLANE)] for first in range(0, count, PLANE)]


def z_groups():
    count = lax.axis_size(AXIS)
    return [[first + f for first in range(0, count, PLANE)] for f in range(PLANE)]


def plane_exchange(blocks):
    return lax.all_to_all(blocks, AXIS, 0, 0, axis_index_groups=plane_groups(), tiled=True)


def z_gather(value):
    return lax.all_gather(value, AXIS, axis_index_groups=z_groups(), axis=0, tiled=True)


def z_reduce(partial):
    return lax.psum_scatter(
        partial.astype(BF), AXIS, axis_index_groups=z_groups(), scatter_dimension=0, tiled=True
    )


def after(value, earlier):
    return lax.optimization_barrier((value, earlier))[0]


def key_block(core, u):
    side = (u & 1) ^ core
    return jnp.where(u >= 0, (u >> 1) + 4 * side, PLANE + ((u + 8) >> 1) - 2 + 2 * side)


def masked_pair(rows):
    lane = lax.broadcasted_iota(jnp.int32, rows.shape, 1)
    zero = jnp.zeros_like(rows)
    first = lane < HEAD_DIM
    return jnp.concatenate([jnp.where(first, rows, zero), jnp.where(first, zero, rows)], 0)


def unpair(both, rows):
    lane = lax.broadcasted_iota(jnp.int32, (rows, both.shape[1]), 1)
    return jnp.where(lane < HEAD_DIM, both[:rows], both[rows:])


def block_probs(core, b, qkv_ref, kv_ref, start_ref):
    rows = qkv_ref.shape[1]
    t = 2 * (b & 3) + (core ^ (b >> 2))
    scaled = (qkv_ref[b, :, 0:128].astype(F32) * HEAD_DIM ** (-0.5)).astype(BF)
    q2 = masked_pair(scaled)
    start = start_ref[b]
    lane = lax.broadcasted_iota(jnp.int32, (rows, 128), 1)
    row = lax.broadcasted_iota(jnp.int32, (rows, 128), 0)
    tiles = []
    places = []
    for j in range(REACH + 1):
        u = t - REACH + j
        at = key_block(core, u)
        places.append(at)
        key_pos = u * 128 + lane
        visible = (key_pos >= start) & (key_pos <= t * 128 + row)
        visible = jnp.concatenate([visible, visible], 0)
        tiles.append(jnp.where(visible, mm_nt(q2, kv_ref[at, :, 0:128]), MASKED))
    scores = jnp.concatenate(tiles, 1)
    top = jnp.max(scores, axis=-1, keepdims=True)
    weights = jnp.exp(scores - top)
    total = jnp.sum(weights, axis=-1, keepdims=True)
    return (places, q2, weights * (1.0 / total))


def attend_kernel(core_ref, qkv_ref, kv_ref, start_ref, out_ref):
    core = core_ref[0]
    rows = qkv_ref.shape[1]

    def body(b, carry):
        places, _, probs = block_probs(core, b, qkv_ref, kv_ref, start_ref)
        probs_b = probs.astype(BF)
        both = jnp.zeros((2 * rows, 128), F32)
        for j, at in enumerate(places):
            both = both + mm(probs_b[:, j * 128 : (j + 1) * 128], kv_ref[at, :, 128:256])
        out_ref[b] = unpair(both, rows).astype(BF)
        return carry

    lax.fori_loop(0, PLANE, body, 0)


def attend_back_kernel(core_ref, qkv_ref, kv_ref, start_ref, grad_ref, dq_ref, dkv_ref):
    core = core_ref[0]
    rows = qkv_ref.shape[1]
    dkv_ref[...] = jnp.zeros_like(dkv_ref)

    def body(b, carry):
        places, q2, probs = block_probs(core, b, qkv_ref, kv_ref, start_ref)
        g2 = masked_pair(grad_ref[b])
        grad_probs = jnp.concatenate(
            [mm_nt(g2, kv_ref[at, :, 128:256]) for at in places], 1
        )
        delta = jnp.sum(probs * grad_probs, axis=-1, keepdims=True)
        grad_scores = (probs * (grad_probs - delta)).astype(BF)
        probs_b = probs.astype(BF)
        both = jnp.zeros((2 * rows, 128), F32)
        for j, at in enumerate(places):
            part = grad_scores[:, j * 128 : (j + 1) * 128]
            both = both + mm(part, kv_ref[at, :, 0:128])
            dkv_ref[at, :, 0:128] += mm_tn(part, q2)
            dkv_ref[at, :, 128:256] += mm_tn(probs_b[:, j * 128 : (j + 1) * 128], g2)
        dq_ref[b] = unpair(both, rows) * HEAD_DIM ** (-0.5)
        return carry

    lax.fori_loop(0, PLANE, body, 0)


def vmem_call(kernel, outs, args):
    return pl.pallas_call(
        kernel,
        out_shape=outs,
        in_specs=[pl.BlockSpec(memory_space=pltpu.SMEM)]
        + [pl.BlockSpec(memory_space=pltpu.VMEM)] * (len(args) - 1),
        out_specs=[pl.BlockSpec(memory_space=pltpu.VMEM)] * len(outs),
        interpret=INTERPRET,
    )(*args)


def local_plane(
    block_input,
    ln1_gain,
    ln1_bias,
    w_qkv,
    bias_qv,
    w_out,
    bias_out,
    ln2_gain,
    ln2_bias,
    w_fc,
    bias_fc,
    w_proj,
    bias_proj,
    seq_lengths,
    out_grad,
):
    count = lax.axis_size(AXIS)
    planes = count // PLANE
    device = lax.axis_index(AXIS)
    z = device // PLANE
    f = device % PLANE
    core = device & 1
    rows, width = block_input.shape
    tokens = PLANE * rows
    share = width // count
    part = width // PLANE
    core_scalar = core.astype(jnp.int32).reshape(1)

    vectors = [ln1_gain, ln1_bias, bias_out, ln2_gain, ln2_bias, bias_proj, bias_qv, bias_fc]
    packed = jnp.concatenate([vector.astype(F32) for vector in vectors]).astype(BF)
    lanes = packed.shape[0]
    qkv_blocks = w_qkv.reshape(share, 3, PLANE, part).transpose(2, 0, 1, 3)
    fc_blocks = w_fc.reshape(share, planes, PLANE, -1).transpose(2, 0, 1, 3)
    hidden = planes * fc_blocks.shape[3]
    slices = jnp.concatenate(
        [
            qkv_blocks.reshape(PLANE, share, 3 * part),
            fc_blocks.reshape(PLANE, share, hidden),
        ],
        axis=2,
    )
    extra = jnp.pad(packed.reshape(1, 1, lanes), ((0, 0), (0, 7), (0, slices.shape[2] - lanes)))
    extra = jnp.broadcast_to(extra, (PLANE, 8, slices.shape[2]))
    arrived = plane_exchange(jnp.concatenate([slices, extra], axis=1))

    row_mean = jnp.mean(block_input, axis=-1, keepdims=True)
    centred = block_input - row_mean
    inverse_one = lax.rsqrt(jnp.mean(centred * centred, axis=-1, keepdims=True) + EPSILON)
    normed_one = centred * inverse_one
    normed_all = plane_gather(normed_one.astype(BF))

    first = z_gather(arrived[:, :, : 3 * part].reshape(-1, 3 * part))
    first = first.reshape(count, share + 8, 3 * part)
    w_qkv_all = first[:, :share].reshape(width, 3 * part)
    vectors = first[:, share, :lanes]

    w_out_column = z_gather(w_out).reshape(planes, share, width)
    og_all = lax.all_gather(
        after(out_grad.astype(BF), arrived),
        AXIS,
        axis_index_groups=plane_groups(),
        axis=0,
        tiled=True,
    ).reshape(PLANE // 2, 2, rows, width)
    w_fc_here = arrived[:, :share, 3 * part :].reshape(PLANE * share, hidden)
    w_fc_all = z_gather(after(w_fc_here, w_qkv_all))

    def whole(i):
        return vectors[:, i * share : (i + 1) * share].reshape(width).astype(F32)

    gain_one, shift_one, b_out, gain_two, shift_two, b_proj = [whole(i) for i in range(6)]
    qv_at = 6 * share
    fc_at = qv_at + bias_qv.shape[0]
    b_qv = vectors[:, qv_at:fc_at].reshape(2, PLANE, part)
    b_qv = lax.dynamic_index_in_dim(b_qv, f, 1, keepdims=False).astype(F32)
    b_fc = vectors[:, fc_at:].reshape(planes, PLANE, -1)
    b_fc = lax.dynamic_index_in_dim(b_fc, f, 1, keepdims=False).reshape(-1).astype(F32)
    b_qkv = jnp.concatenate([b_qv[0], jnp.zeros((part,), F32), b_qv[1]])

    act_one = [
        (half.astype(F32) * gain_one + shift_one).astype(BF) for half in halves(normed_all)
    ]
    qkv = jnp.concatenate([(mm(half, w_qkv_all) + b_qkv).astype(BF) for half in act_one])
    qkv = qkv.reshape(PLANE, rows, 3 * part)
    kv_own = qkv[:, :, part:]
    kv_late = kv_own.reshape(2, 4, rows, 2 * part)[:, 2:].reshape(4, rows, 2 * part)
    kv_before = from_behind(kv_late, AXIS, PLANE)
    kv_all = jnp.concatenate([kv_own, kv_before])
    block = jnp.arange(PLANE, dtype=jnp.int32)
    order = 2 * (block & 3) + (core ^ (block >> 2))
    positions = (z * tokens + order * rows)[:, None] + jnp.arange(rows, dtype=jnp.int32)[None]
    seq_starts = jnp.cumsum(seq_lengths) - seq_lengths
    token_start = jnp.max(
        jnp.where(seq_starts <= positions[:, :, None], seq_starts, 0), axis=2, keepdims=True
    )
    begins = (token_start - z * tokens).astype(jnp.int32)
    w_proj_all = z_gather(after(w_proj, qkv))
    w_out_column = after(w_out_column, qkv)
    w_out_all = plane_exchange(jnp.repeat(w_out_column, 2, axis=0))
    w_out_all = lax.dynamic_slice_in_dim(w_out_all, 4 * core, 4, 0).reshape(part, width)
    (mixed,) = vmem_call(
        attend_kernel,
        [jax.ShapeDtypeStruct((PLANE, rows, part), BF)],
        (core_scalar, qkv, kv_all, begins),
    )
    mixed = halves((mixed[:4], mixed[4:]))
    out_sum = chip_fold(core_fold(*[mm(half, w_out_all) for half in mixed]))
    hidden_res = block_input + out_sum + b_out
    normed_two, inverse_two, affine_two = layer_norm(hidden_res, gain_two, shift_two)
    act_two = halves(plane_gather(affine_two.astype(BF)))
    og = [
        lax.dynamic_index_in_dim(og_all, side, 1, keepdims=False).reshape(-1, width)
        for side in (core, 1 - core)
    ]
    pairs = [gelu_pair(mm(half, w_fc_all) + b_fc) for half in act_two]
    gelu_out = [activated.astype(BF) for activated, _ in pairs]

    grad_pre = [mm_nt(half, w_proj_all) * pair[1] for half, pair in zip(og, pairs)]
    grad_pre_b = [half.astype(BF) for half in grad_pre]
    partial_two = [mm_nt(half, w_fc_all) for half in grad_pre_b]
    gelu_late, pre_late, act_late, partial_two = lax.optimization_barrier(
        (gelu_out, grad_pre_b, act_two, partial_two)
    )
    kept_two = core_fold(*partial_two)
    grad_act_two = chip_fold(kept_two)
    fc_part = (mm_tn(act_late[0], pre_late[0]) + mm_tn(act_late[1], pre_late[1])).astype(BF)
    proj_part = (mm_tn(gelu_late[0], og[0]) + mm_tn(gelu_late[1], og[1])).astype(BF)
    grad_w_fc_here = z_reduce(fc_part)
    grad_w_proj = z_reduce(proj_part).astype(F32)
    proj_terms = [mm(half, w_proj_all) for half in gelu_late]
    kept_proj = core_fold(*proj_terms)
    grad_fc_bias = jnp.sum(grad_pre[0], axis=0) + jnp.sum(grad_pre[1], axis=0)
    grad_hidden = out_grad + norm_back(grad_act_two, gain_two, normed_two, inverse_two)
    grad_hidden_b = halves(plane_gather(grad_hidden.astype(BF)))
    grad_mixed = jnp.concatenate([mm_nt(half, w_out_all).astype(BF) for half in grad_hidden_b])
    grad_mixed, fc_part, proj_part, kept_proj = lax.optimization_barrier(
        (grad_mixed, fc_part, proj_part, kept_proj)
    )
    grad_mixed = grad_mixed.reshape(PLANE, rows, part)
    proj_sum = chip_fold(kept_proj)
    block_output = hidden_res + proj_sum + b_proj

    grad_queries, grad_kv_all = vmem_call(
        attend_back_kernel,
        [
            jax.ShapeDtypeStruct((PLANE, rows, part), F32),
            jax.ShapeDtypeStruct((PLANE + 4, rows, 2 * part), F32),
        ],
        (core_scalar, qkv, kv_all, begins, grad_mixed),
    )
    kv_back = from_behind(grad_kv_all[PLANE:].astype(BF), AXIS, -PLANE).astype(F32)
    grad_kv = grad_kv_all[:PLANE].reshape(2, 4, rows, 2 * part)
    kv_back = jnp.pad(kv_back.reshape(2, 2, rows, 2 * part), ((0, 0), (2, 0), (0, 0), (0, 0)))
    grad_kv = (grad_kv + kv_back).reshape(tokens, 2 * part)
    grad_queries = grad_queries.reshape(tokens, part)
    grad_qkv = jnp.concatenate([grad_queries, grad_kv], axis=1)
    qkv_sums = jnp.sum(grad_qkv, axis=0)
    grad_qkv = grad_qkv.astype(BF)
    grad_qkv = [grad_qkv[: tokens // 2], grad_qkv[tokens // 2 :]]
    qkv_part = (mm_tn(act_one[0], grad_qkv[0]) + mm_tn(act_one[1], grad_qkv[1])).astype(BF)
    grad_w_qkv_here = z_reduce(qkv_part)
    grad_qkv = after(grad_qkv, qkv_part)
    partial_one = [mm_nt(half, w_qkv_all) for half in grad_qkv]
    kept_one = core_fold(*partial_one)
    grad_act_one = chip_fold(kept_one)

    mixed = after(mixed, grad_queries)
    out_part = mm_tn(mixed[0], grad_hidden_b[0]) + mm_tn(mixed[1], grad_hidden_b[1])
    out_part = jnp.tile(out_part.astype(BF).reshape((4,) + w_out.shape), (2, 1, 1))
    out_part = plane_exchange(out_part).reshape((4, 2) + w_out.shape)
    out_part = lax.dynamic_index_in_dim(out_part, f // 4, 1, keepdims=False)
    grad_w_out = z_reduce(out_part.reshape(width // PLANE, width))

    leaving = jnp.concatenate([grad_w_qkv_here, grad_w_fc_here], axis=1)
    landed = plane_exchange(leaving.reshape(PLANE, share, 3 * part + hidden))
    grad_w_out = after(grad_w_out, landed).astype(F32)
    landed = landed.astype(F32)
    grad_w_qkv = landed[:, :, : 3 * part].reshape(PLANE, share, 3, part)
    grad_w_qkv = grad_w_qkv.transpose(1, 2, 0, 3).reshape(w_qkv.shape)
    grad_w_fc = landed[:, :, 3 * part :].reshape(PLANE, share, planes, -1)
    grad_w_fc = grad_w_fc.transpose(1, 2, 0, 3).reshape(w_fc.shape)

    grad_input = grad_hidden + norm_back(grad_act_one, gain_one, normed_one, inverse_one)

    normed_halves = [half.astype(F32) for half in halves(normed_all)]
    sums = [
        jnp.sum(partial_one[0] * normed_halves[0], axis=0)
        + jnp.sum(partial_one[1] * normed_halves[1], axis=0),
        jnp.sum(partial_one[0], axis=0) + jnp.sum(partial_one[1], axis=0),
        jnp.sum(grad_hidden, axis=0),
        jnp.sum(grad_act_two * normed_two, axis=0),
        jnp.sum(grad_act_two, axis=0),
        jnp.sum(out_grad, axis=0),
    ]
    qv_sums = jnp.stack([qkv_sums[:part], qkv_sums[2 * part :]])
    here = (jnp.arange(width, dtype=jnp.int32) // part == f)[None]
    qv_terms = jnp.where(here, jnp.tile(qv_sums, (1, PLANE)), 0.0)
    fc_terms = jnp.where(here, jnp.tile(grad_fc_bias.reshape(planes, part), (1, PLANE)), 0.0)
    terms = jnp.concatenate([jnp.stack(sums), qv_terms, fc_terms])
    total = add_everywhere(terms)
    small = pick(total[:6].reshape(6, count, share).transpose(1, 0, 2), device)
    small_qv = pick(total[6:8].reshape(count, -1), device)
    small_fc = pick(total[8:].reshape(count, -1), device)
    return (
        block_output,
        grad_input,
        small[0],
        small[1],
        grad_w_qkv,
        small_qv,
        grad_w_out,
        small[2],
        small[3],
        small[4],
        grad_w_fc,
        small_fc,
        grad_w_proj,
        small[5],
    )


def solution(mesh):
    if mesh.size != 32:
        return planned(mesh, local_any)
    return planned(mesh, local_plane)


def planned(mesh, local):
    return jax.shard_map(
        local,
        mesh=mesh,
        in_specs=(
            P(AXIS, None),
            P(AXIS),
            P(AXIS),
            P(AXIS, None),
            P(AXIS),
            P(AXIS, None),
            P(AXIS),
            P(AXIS),
            P(AXIS),
            P(AXIS, None),
            P(AXIS),
            P(AXIS, None),
            P(AXIS),
            P(),
            P(AXIS, None),
        ),
        out_specs=(
            P(AXIS, None),
            P(AXIS, None),
            P(AXIS),
            P(AXIS),
            P(AXIS, None),
            P(AXIS),
            P(AXIS, None),
            P(AXIS),
            P(AXIS),
            P(AXIS),
            P(AXIS, None),
            P(AXIS),
            P(AXIS, None),
            P(AXIS),
        ),
        check_vma=False,
    )
```
